128 devices in a mesh: slab: 64 (over y, z, x), blk: 2 (over core).
Axes of the slice: x: 4, y: 4, z: 4, core: 2. Of those that a mesh axis runs over, the one named last changes fastest.
Arguments:
- p_blocks: bfloat16 [2, 2048, 64, 64], P('blk', 'slab'), may hold values from -0.75 to 0.75
- basis_vals: bfloat16 [512, 8, 64, 128], P('slab'), may hold values from -0.75 to 0.75
- need_list: int32 [2, 64, 64, 4], P('blk', 'slab'), may hold values from 0 to 31, as said below
- tasks: int32 [2, 64, 4, 1536], P('blk', 'slab'), may hold values from 0 to 255, as said below
- task_counts: int32 [2, 64], P('blk', 'slab'), may hold values from 1 to 1536, as said below
Outputs:
- density: float32 [512, 128], P('slab')
- potential_blocks: float32 [2, 2048, 64, 64], P('blk', 'slab')
The draws below stay inside these ranges and needn't reach their ends.
Inputs may be any that keep to these rules, and one draw needn't show every extreme that they name: The 4 entries of one need_list[c, s, o, :] are distinct. `tasks`: field 0 is below 8, fields 1 and 2 below 8, field 3 below 256. `task_counts`: some device has 1536 live tasks.
All inputs are finite; a program needn't handle non-finite values.
Results may differ from the reference program's by a relative error of at most 0.0029.
Values may be sent and summed in bfloat16 or wider, within the bound.
No kernel may reach another device: no remote copies, remote signals or barrier semaphores. Data moves between devices by JAX's collectives and lax.ppermute only.
A program may use at most 128 MiB of HBM per device.

```python
import jax
import jax.numpy as jnp
from jax import lax

BS = 64
NPT = 128
KLOC = 8
NBAT = 8
TCAP = 1536
BLK_DEV = 32
CAP = 4
SLABS = 64
COLUMNS = 2
BLOCKS = 2048
BATCHES = 512


def draw_need_list(key, part):
    row_lookup_key = jax.random.split(key, COLUMNS * SLABS * SLABS)

    def one_row(row_key):
        return jax.random.permutation(row_key, BLK_DEV)[:CAP]
    rows_all = jax.vmap(one_row)(row_lookup_key)
    return rows_all.reshape(COLUMNS, SLABS, SLABS, CAP).astype(jnp.int32)


def draw_tasks(key, part):
    task_shape = (COLUMNS, SLABS, TCAP)
    batch_field = jax.random.randint(jax.random.fold_in(key, 11), task_shape, 0, NBAT)
    left_field = jax.random.randint(jax.random.fold_in(key, 12), task_shape, 0, KLOC)
    right_field = jax.random.randint(jax.random.fold_in(key, 13), task_shape, 0, KLOC)
    slot_field = jax.random.randint(jax.random.fold_in(key, 14), task_shape, 0, SLABS * CAP)
    return jnp.stack([batch_field, left_field, right_field, slot_field], axis=2).astype(jnp.int32)


def draw_task_counts(key, part):
    drawn_counts = jax.random.randint(jax.random.fold_in(key, 21), (COLUMNS * SLABS,), max(TCAP // 4, 1), TCAP + 1)
    busiest = jax.random.randint(jax.random.fold_in(key, 22), (), 0, COLUMNS * SLABS)
    positions = jnp.arange(COLUMNS * SLABS, dtype=jnp.int32)
    counts_all = jnp.where(positions == busiest, TCAP, drawn_counts)
    return counts_all.reshape(COLUMNS, SLABS).astype(jnp.int32)


def block_levels(key, shape, shards, least, top_value):
    level = 1.0
    for position, shards_of in shards:
        steps = jax.random.uniform(jax.random.fold_in(jax.random.fold_in(key, 6), position), (shards_of,), jnp.float32, least / len(shards), top_value / len(shards))
        level = level * jnp.repeat(jnp.exp(steps), shape[position] // shards_of).reshape((-1,) + (1,) * (len(shape) - 1 - position))
    return level


def scatter_about(key, extent, width, most, shards=(), kind=jnp.bfloat16):
    array = jax.random.normal(key, extent, jnp.float32) * width
    if len(shards) > 0:
        array = block_levels(key, extent, shards, -0.22, 0.18) * array
    return jnp.clip(array, min=-most, max=most).astype(kind)


def setup_inputs(seed: int = 0) -> dict:
    splits = jax.random.split(jax.random.key(seed), 6)
    return {
        "p_blocks": scatter_about(splits[0], (COLUMNS, BLOCKS, BS, BS), BS ** -0.5, 0.75, ((0, 2), (1, 64))),
        "basis_vals": scatter_about(splits[1], (BATCHES, KLOC, BS, NPT), (BS ** -0.5), 0.75, ((0, 64),)),
        "need_list": draw_need_list(jax.random.fold_in(splits[5], 71), 0),
        "tasks": draw_tasks(jax.random.fold_in(splits[5], 71), 0),
        "task_counts": draw_task_counts(jax.random.fold_in(splits[5], 71), 0),
    }


def task_terms(p_blocks, basis_vals, need_list, tasks, task_counts, device):
    column = device // SLABS
    slab_index = device % SLABS
    offsets = jnp.arange(SLABS, dtype=jnp.int32)[:, None] * BLK_DEV
    global_ids = (offsets + need_list[column, slab_index]).reshape(-1).astype(jnp.int32)
    received = p_blocks[column][global_ids]
    task_fields = tasks[column, slab_index]
    grid_batch_index = (task_fields[0] + slab_index * NBAT).astype(jnp.int32)
    live_mask = (jnp.arange(TCAP, dtype=jnp.int32) < task_counts[column, slab_index]).astype(jnp.float32)
    left_vals = basis_vals[grid_batch_index, task_fields[1]]
    right_side_values = basis_vals[grid_batch_index, task_fields[2]]
    selected_entries = received[task_fields[3]]
    return (column, global_ids, grid_batch_index, live_mask, left_vals, right_side_values, selected_entries, task_fields[3])

def reference(p_blocks, basis_vals, need_list, tasks, task_counts):

    def add_density(total, device):
        column, global_ids, grid_batch_index, live_mask, left_vals, right_side_values, selected_entries, slot_ids = task_terms(p_blocks, basis_vals, need_list, tasks, task_counts, device)
        mapped_result = jnp.einsum('zhf,zfx->zhx', selected_entries.astype(jnp.float32), right_side_values.astype(jnp.float32))
        contrib = lax.optimization_barrier(jnp.sum(left_vals.astype(jnp.float32) * mapped_result, axis=1)) * live_mask[:, None]
        return (total.at[grid_batch_index].add(contrib), None)
    devices_all = jnp.arange(COLUMNS * SLABS, dtype=jnp.int32)
    density, _ = lax.scan(add_density, jnp.zeros((BATCHES, NPT), jnp.float32), devices_all)
    potential = density / jnp.sqrt(1.0 + density * density)

    def add_potential(total, device):
        column, global_ids, grid_batch_index, live_mask, left_vals, right_side_values, selected_entries, slot_ids = task_terms(p_blocks, basis_vals, need_list, tasks, task_counts, device)
        weight_applied = (left_vals.astype(jnp.float32) * potential[grid_batch_index][:, None, :]).astype(jnp.bfloat16)
        incomplete_sum_terms = jnp.einsum('lkf,lgf->lkg', weight_applied.astype(jnp.float32), right_side_values.astype(jnp.float32))
        incomplete_sum_terms = incomplete_sum_terms * live_mask[:, None, None]
        slot_sums = jnp.zeros((SLABS * CAP, BS, BS), jnp.float32).at[slot_ids].add(incomplete_sum_terms)
        return (total.at[column, global_ids].add(slot_sums), None)
    potential_blocks, _ = lax.scan(add_potential, jnp.zeros((COLUMNS, BLOCKS, BS, BS), jnp.float32), devices_all)
    return (density, potential_blocks)
```

```python
import functools

import jax
import jax.numpy as jnp
from jax import lax
from jax.experimental import pallas as pl
from jax.experimental.pallas import tpu as pltpu
from jax.sharding import PartitionSpec as P

F32 = jnp.float32
BF16 = jnp.bfloat16
LANES = 128
SUB = 8
CHUNK = 512


def dot_nn(a, b):
    return lax.dot_general(a, b, (((1,), (0,)), ((), ())), preferred_element_type=F32)


def dot_nt(a, b):
    return lax.dot_general(a, b, (((1,), (1,)), ((), ())), preferred_element_type=F32)


def dot_tn(a, b):
    return lax.dot_general(a, b, (((0,), (0,)), ((), ())), preferred_element_type=F32)


def split_pair(x):
    hi = x.astype(BF16)
    return hi, (x - hi.astype(F32)).astype(BF16)


def prep_kernel(count_ref, tasks_ref, v_ref, c_ref, ct_ref, v2_ref, flag_ref):
    nbat, kloc, bs, npt = v_ref.shape
    keys = nbat * kloc * kloc
    slots = c_ref.shape[2]
    tcap = tasks_ref.shape[1]
    step = CHUNK if tcap % CHUNK == 0 else tcap
    live = count_ref[0, 0]
    c = jnp.zeros((keys, slots), F32)
    ct = jnp.zeros((slots, keys), F32)
    for t in range(0, tcap, step):
        fields = tasks_ref[:, t : t + step]
        key = (fields[0:1] * kloc + fields[2:3]) * kloc + fields[1:2]
        lane = lax.broadcasted_iota(jnp.int32, (1, step), 1) + t
        key = jnp.where(lane < live, key, -1)
        key_hot = jnp.where(
            lax.broadcasted_iota(jnp.int32, (keys, step), 0) == key, 1.0, 0.0
        ).astype(BF16)
        slot_hot = jnp.where(
            lax.broadcasted_iota(jnp.int32, (slots, step), 0) == fields[3:4], 1.0, 0.0
        ).astype(BF16)
        c += dot_nt(key_hot, slot_hot)
        ct += dot_nt(slot_hot, key_hot)
    c_hi = jnp.floor(c * (1.0 / 256.0)) * 256.0
    ct_hi = jnp.floor(ct * (1.0 / 256.0)) * 256.0
    c_ref[0] = (c - c_hi).astype(BF16)
    c_ref[1] = c_hi.astype(BF16)
    ct_ref[0] = (ct - ct_hi).astype(BF16)
    ct_ref[1] = ct_hi.astype(BF16)
    flag_ref[0, 0] = jnp.where(jnp.max(c) > 255.5, 1, 0).astype(jnp.int32)
    half = bs // 2
    for b in range(nbat):
        vals = jnp.swapaxes(v_ref[b].astype(F32), 0, 1)
        for h in range(2):
            part = vals[h * half : (h + 1) * half].reshape(half * kloc, npt)
            v2_ref[b, :, h * npt : (h + 1) * npt] = part.astype(BF16)


def send_kernel(req_ref, own_ref, o_ref):
    nblk, bs, _ = own_ref.shape
    half = bs // 2
    slabs, _, cap, _ = o_ref.shape
    slots = slabs * cap
    own = own_ref[...].astype(F32)
    own = jnp.concatenate([own[:, :half], own[:, half:]], axis=2)
    own = jnp.swapaxes(own, 0, 1).astype(BF16)
    hot = jnp.where(
        lax.broadcasted_iota(jnp.int32, (nblk, slots), 0) == req_ref[...], 1.0, 0.0
    ).astype(BF16)
    for jp in range(half // 2):
        rhs = jnp.concatenate([own[2 * jp], own[2 * jp + 1]], axis=1)
        res = dot_tn(hot, rhs).astype(BF16)
        o_ref[:, 2 * jp] = res[:, :LANES].reshape(slabs, cap, LANES)
        o_ref[:, 2 * jp + 1] = res[:, LANES:].reshape(slabs, cap, LANES)


def fill_values(bd_ref, v_ref, b, kloc, bs):
    for l in range(kloc):
        v = v_ref[b, l]
        bd_ref[l * LANES : l * LANES + bs, 0:LANES] = v
        bd_ref[l * LANES + bs : (l + 1) * LANES, LANES:] = v


def density_kernel(flag_ref, r_ref, c_ref, v_ref, v2_ref, d_ref, res, hi_s, lo_s, bd):
    nbat, kloc, bs, npt = v_ref.shape
    half = bs // 2
    slabs, _, cap, _ = r_ref.shape
    slots = slabs * cap

    def build(jp, carry):
        r0 = r_ref[:, 2 * jp].reshape(slots, LANES)
        r1 = r_ref[:, 2 * jp + 1].reshape(slots, LANES)
        rhs = jnp.concatenate([r0, r1], axis=1)
        res[...] = dot_nn(c_ref[0], rhs)

        @pl.when(flag_ref[0, 0] > 0)
        def _():
            res[...] += dot_nn(c_ref[1], rhs)

        row = pl.multiple_of(jp * 2 * SUB, 2 * SUB)
        for b in range(nbat):
            for l in range(kloc):
                r = (b * kloc + l) * SUB
                x = jnp.concatenate(
                    [res[r : r + SUB, :LANES], res[r : r + SUB, LANES:]], axis=0
                )
                hi, lo = split_pair(x)
                hi_s[b, pl.ds(row, 2 * SUB), l * LANES : (l + 1) * LANES] = hi
                lo_s[b, pl.ds(row, 2 * SUB), l * LANES : (l + 1) * LANES] = lo
        return carry

    lax.fori_loop(0, half // 2, build, 0)
    bd[...] = jnp.zeros_like(bd)

    def one_batch(b, carry):
        fill_values(bd, v_ref, b, kloc, bs)
        values = bd[...]
        image = dot_nn(hi_s[b], values) + dot_nn(lo_s[b], values)
        d = jnp.sum(image * v2_ref[b].astype(F32), axis=0, keepdims=True)
        d_ref[pl.ds(b, 1), :] = d[:, :npt] + d[:, npt:]
        return carry

    lax.fori_loop(0, nbat, one_batch, 0)


def potential_kernel(flag_ref, d_ref, ct_ref, v_ref, v2_ref, o_ref, g, hi_s, lo_s, bd):
    nbat, kloc, bs, npt = v_ref.shape
    half = bs // 2
    slabs, _, cap, _ = o_ref.shape
    bd[...] = jnp.zeros_like(bd)

    def one_batch(b, carry):
        fill_values(bd, v_ref, b, kloc, bs)
        d = d_ref[pl.ds(b, 1), :]
        pot = d / jnp.sqrt(1.0 + d * d)
        pot2 = jnp.concatenate([pot, pot], axis=1)
        weighted = (v2_ref[b].astype(F32) * pot2).astype(BF16)
        g[...] = dot_nt(weighted, bd[...])
        for lp in range(kloc // 2):
            row = pl.multiple_of((b * kloc + 2 * lp) * SUB, 2 * SUB)
            for j in range(half):
                x = jnp.concatenate(
                    [
                        g[j * SUB : (j + 1) * SUB, 2 * lp * LANES : (2 * lp + 1) * LANES],
                        g[j * SUB : (j + 1) * SUB, (2 * lp + 1) * LANES : (2 * lp + 2) * LANES],
                    ],
                    axis=0,
                )
                hi, lo = split_pair(x)
                hi_s[pl.ds(row, 2 * SUB), j * LANES : (j + 1) * LANES] = hi
                lo_s[pl.ds(row, 2 * SUB), j * LANES : (j + 1) * LANES] = lo
        return carry

    lax.fori_loop(0, nbat, one_batch, 0)
    for jp in range(half // 2):
        cols = slice(2 * jp * LANES, (2 * jp + 2) * LANES)

        def sums(n):
            return dot_nn(ct_ref[n], hi_s[:, cols]) + dot_nn(ct_ref[n], lo_s[:, cols])

        out = lax.cond(flag_ref[0, 0] > 0, lambda: sums(0) + sums(1), lambda: sums(0))
        out = out.astype(BF16)
        o_ref[:, 2 * jp] = out[:, :LANES].reshape(slabs, cap, LANES)
        o_ref[:, 2 * jp + 1] = out[:, LANES:].reshape(slabs, cap, LANES)


def owner_kernel(req_ref, ret_ref, o_ref):
    nblk, bs, _ = o_ref.shape
    half = bs // 2
    slabs, _, cap, _ = ret_ref.shape
    slots = slabs * cap
    hot = jnp.where(
        lax.broadcasted_iota(jnp.int32, (nblk, slots), 0) == req_ref[...], 1.0, 0.0
    ).astype(BF16)
    parts = []
    for jp in range(half // 2):
        r0 = ret_ref[:, 2 * jp].reshape(slots, LANES)
        r1 = ret_ref[:, 2 * jp + 1].reshape(slots, LANES)
        res = dot_nn(hot, jnp.concatenate([r0, r1], axis=1))
        parts += [res[:, :LANES], res[:, LANES:]]
    sums = jnp.swapaxes(jnp.stack(parts, axis=0), 0, 1)
    o_ref[:, :half] = sums[:, :, :bs]
    o_ref[:, half:] = sums[:, :, bs:]


SMEM = pl.BlockSpec(memory_space=pltpu.SMEM)
VMEM = pl.BlockSpec(memory_space=pltpu.VMEM)


def body(p_blocks, basis_vals, need_list, tasks, task_counts):
    own = p_blocks[0]
    blk_dev, bs, _ = own.shape
    nbat, kloc, _, npt = basis_vals.shape
    slabs, cap = need_list.shape[2:]
    slots = slabs * cap
    half = bs // 2
    keys = nbat * kloc * kloc
    wide = (slabs, half, cap, LANES)
    vmem_limit = pltpu.CompilerParams(vmem_limit_bytes=56 << 20)

    requested = lax.all_to_all(need_list[0, 0], "slab", split_axis=0, concat_axis=0, tiled=True)
    requested = requested.reshape(1, slots)

    counts, counts_t, v2, flag = pl.pallas_call(
        prep_kernel,
        out_shape=(
            jax.ShapeDtypeStruct((2, keys, slots), BF16),
            jax.ShapeDtypeStruct((2, slots, keys), BF16),
            jax.ShapeDtypeStruct((nbat, half * kloc, 2 * npt), BF16),
            jax.ShapeDtypeStruct((1, 1), jnp.int32),
        ),
        in_specs=[SMEM, VMEM, VMEM],
        out_specs=(VMEM, VMEM, VMEM, SMEM),
        compiler_params=vmem_limit,
        name="prep",
    )(task_counts, tasks[0, 0], basis_vals)

    sends = pl.pallas_call(
        send_kernel,
        out_shape=jax.ShapeDtypeStruct(wide, BF16),
        in_specs=[VMEM, VMEM],
        out_specs=VMEM,
        compiler_params=vmem_limit,
        name="send",
    )(requested, own)
    received = lax.all_to_all(sends, "slab", split_axis=0, concat_axis=0, tiled=True)

    partial = pl.pallas_call(
        density_kernel,
        out_shape=jax.ShapeDtypeStruct((nbat, npt), F32),
        in_specs=[SMEM, VMEM, VMEM, VMEM, VMEM],
        out_specs=VMEM,
        scratch_shapes=[
            pltpu.VMEM((keys, 2 * LANES), F32),
            pltpu.VMEM((nbat, half * kloc, kloc * LANES), BF16),
            pltpu.VMEM((nbat, half * kloc, kloc * LANES), BF16),
            pltpu.VMEM((kloc * LANES, 2 * LANES), BF16),
        ],
        compiler_params=vmem_limit,
        name="density",
    )(flag, received, counts, basis_vals, v2)
    density = lax.psum(partial, "blk")

    slot_sums = pl.pallas_call(
        potential_kernel,
        out_shape=jax.ShapeDtypeStruct(wide, BF16),
        in_specs=[SMEM, VMEM, VMEM, VMEM, VMEM],
        out_specs=VMEM,
        scratch_shapes=[
            pltpu.VMEM((half * kloc, kloc * LANES), F32),
            pltpu.VMEM((keys, half * LANES), BF16),
            pltpu.VMEM((keys, half * LANES), BF16),
            pltpu.VMEM((kloc * LANES, 2 * LANES), BF16),
        ],
        compiler_params=vmem_limit,
        name="potential",
    )(flag, density, counts_t, basis_vals, v2)
    returned = lax.all_to_all(slot_sums, "slab", split_axis=0, concat_axis=0, tiled=True)

    owner_sums = pl.pallas_call(
        owner_kernel,
        out_shape=jax.ShapeDtypeStruct((blk_dev, bs, bs), F32),
        in_specs=[VMEM, VMEM],
        out_specs=VMEM,
        compiler_params=vmem_limit,
        name="owner",
    )(requested, returned)
    return (density, owner_sums[None])


def solution(mesh):
    in_specs = (
        P("blk", "slab", None, None),
        P("slab", None, None, None),
        P("blk", "slab", None, None),
        P("blk", "slab", None, None),
        P("blk", "slab"),
    )
    out_specs = (P("slab", None), P("blk", "slab", None, None))
    return jax.shard_map(body, mesh=mesh, in_specs=in_specs, out_specs=out_specs, check_vma=False)
```

```python
import functools

import jax
import jax.numpy as jnp
from jax import lax
from jax.experimental import pallas as pl
from jax.experimental.pallas import tpu as pltpu
from jax.sharding import PartitionSpec as P

F32 = jnp.float32
BF16 = jnp.bfloat16
LANES = 128
SUB = 8
TASK_STEP = 512
PARTS = 2


def dot_nn(a, b):
    return lax.dot_general(a, b, (((1,), (0,)), ((), ())), preferred_element_type=F32)


def dot_nt(a, b):
    return lax.dot_general(a, b, (((1,), (1,)), ((), ())), preferred_element_type=F32)


def dot_tn(a, b):
    return lax.dot_general(a, b, (((0,), (0,)), ((), ())), preferred_element_type=F32)


def split_pair(x):
    hi = x.astype(BF16)
    return hi, (x - hi.astype(F32)).astype(BF16)


def own_kernel(own_ref, o_ref):
    half = own_ref.shape[1] // 2
    own = own_ref[...].astype(F32)
    own = jnp.concatenate([own[:, :half], own[:, half:]], axis=2)
    own = jnp.swapaxes(own, 0, 1).astype(BF16)
    for j in range(half):
        o_ref[j // 2, :, (j % 2) * LANES : (j % 2 + 1) * LANES] = own[j]


def prep_kernel(count_ref, tasks_ref, v_ref, c_ref, ct_ref, v2_ref, flag_ref):
    nbat, kloc, bs, npt = v_ref.shape
    keys = nbat * kloc * kloc
    slots = c_ref.shape[2]
    tcap = tasks_ref.shape[1]
    step = TASK_STEP if tcap % TASK_STEP == 0 else tcap
    live = count_ref[0, 0]
    c = jnp.zeros((keys, slots), F32)
    ct = jnp.zeros((slots, keys), F32)
    for t in range(0, tcap, step):
        fields = tasks_ref[:, t : t + step]
        key = (fields[0:1] * kloc + fields[2:3]) * kloc + fields[1:2]
        lane = lax.broadcasted_iota(jnp.int32, (1, step), 1) + t
        key = jnp.where(lane < live, key, -1)
        key_hot = jnp.where(
            lax.broadcasted_iota(jnp.int32, (keys, step), 0) == key, 1.0, 0.0
        ).astype(BF16)
        slot_hot = jnp.where(
            lax.broadcasted_iota(jnp.int32, (slots, step), 0) == fields[3:4], 1.0, 0.0
        ).astype(BF16)
        c += dot_nt(key_hot, slot_hot)
        ct += dot_nt(slot_hot, key_hot)
    c_hi = jnp.floor(c * (1.0 / 256.0)) * 256.0
    ct_hi = jnp.floor(ct * (1.0 / 256.0)) * 256.0
    c_ref[0] = (c - c_hi).astype(BF16)
    c_ref[1] = c_hi.astype(BF16)
    ct_ref[0] = (ct - ct_hi).astype(BF16)
    ct_ref[1] = ct_hi.astype(BF16)
    flag_ref[0, 0] = jnp.where(jnp.max(c) > 255.5, 1, 0).astype(jnp.int32)
    half = bs // 2
    for b in range(nbat):
        vals = jnp.swapaxes(v_ref[b].astype(F32), 0, 1)
        for h in range(2):
            part = vals[h * half : (h + 1) * half].reshape(half * kloc, npt)
            v2_ref[b, :, h * npt : (h + 1) * npt] = part.astype(BF16)


def request_hot(req_ref, nblk):
    slabs, _, cap = req_ref.shape
    slots = slabs * cap
    req = req_ref[...].reshape(slabs, cap).astype(F32).astype(BF16)
    row = lax.broadcasted_iota(jnp.int32, (slots, slabs), 0) // cap
    col = lax.broadcasted_iota(jnp.int32, (slots, slabs), 1)
    spread = dot_nn(jnp.where(row == col, 1.0, 0.0).astype(BF16), req)
    nth = lax.broadcasted_iota(jnp.int32, (slots, cap), 0) % cap
    keep = lax.broadcasted_iota(jnp.int32, (slots, cap), 1) == nth
    ids = jnp.sum(jnp.where(keep, spread, 0.0), axis=1, keepdims=True).astype(jnp.int32)
    ids = jnp.broadcast_to(ids, (slots, nblk))
    same = lax.broadcasted_iota(jnp.int32, (slots, nblk), 1) == ids
    return jnp.where(same, 1.0, 0.0).astype(BF16)


def send_rows(hot, own_ref, o_ref, first):
    slabs, rows, cap, _ = o_ref.shape
    for jp in range(rows // 2):
        res = dot_nn(hot, own_ref[first // 2 + jp]).astype(BF16)
        o_ref[:, 2 * jp] = res[:, :LANES].reshape(slabs, cap, LANES)
        o_ref[:, 2 * jp + 1] = res[:, LANES:].reshape(slabs, cap, LANES)


def first_send_kernel(req_ref, own_ref, o_ref, hot_ref):
    hot = request_hot(req_ref, own_ref.shape[1])
    hot_ref[...] = hot
    send_rows(hot, own_ref, o_ref, 0)


def next_send_kernel(hot_ref, own_ref, o_ref, *, first):
    send_rows(hot_ref[...], own_ref, o_ref, first)


def slot_rows(ref, jp):
    slabs, _, cap, _ = ref.shape
    r0 = ref[:, 2 * jp].reshape(slabs * cap, LANES)
    r1 = ref[:, 2 * jp + 1].reshape(slabs * cap, LANES)
    return jnp.concatenate([r0, r1], axis=1)


def diagonal_values(v_ref, b):
    _, kloc, bs, npt = v_ref.shape
    zero = jnp.zeros((bs, npt), BF16)
    rows = []
    for l in range(kloc):
        v = v_ref[b, l]
        rows.append(jnp.concatenate([v, zero], axis=1))
        rows.append(jnp.concatenate([zero, v], axis=1))
    return jnp.concatenate(rows, axis=0)


def density_kernel(flag_ref, r_ref, c_ref, v_ref, v2_ref, d0_ref, d_ref, hi_s, lo_s, *, first):
    nbat, kloc, _, npt = v_ref.shape
    rows = r_ref.shape[1]
    keys, slots = c_ref.shape[1:]

    def build(jp, parts):
        rhs = slot_rows(r_ref, jp)
        res = dot_nn(c_ref[0], rhs)
        if parts == 2:
            res += dot_nn(c_ref[1], rhs)
        res = res.reshape(keys // SUB, SUB, 2 * LANES)
        hi, lo = split_pair(jnp.concatenate([res[:, :, :LANES], res[:, :, LANES:]], axis=1))
        at = pl.ds(pl.multiple_of(jp * 2 * SUB, 2 * SUB), 2 * SUB)
        hi_s[:, at, :] = hi
        lo_s[:, at, :] = lo

    def loop(parts, unroll):
        def step(jp, carry):
            build(jp, parts)
            return carry

        lax.fori_loop(0, rows // 2, step, 0, unroll=unroll)

    @pl.when(flag_ref[0, 0] == 0)
    def _():
        loop(1, 2)

    @pl.when(flag_ref[0, 0] != 0)
    def _():
        loop(2, 1)

    def one_batch(b, carry):
        lhs = jnp.concatenate(
            [
                jnp.concatenate([hi_s[b * kloc + l] for l in range(kloc)], axis=1),
                jnp.concatenate([lo_s[b * kloc + l] for l in range(kloc)], axis=1),
            ],
            axis=0,
        )
        image = dot_nn(lhs, diagonal_values(v_ref, b))
        image = image[: rows * SUB] + image[rows * SUB :]
        left = v2_ref[b, first * SUB : (first + rows) * SUB].astype(F32)
        d = jnp.sum(image * left, axis=0, keepdims=True)
        d_ref[pl.ds(b, 1), :] = d0_ref[pl.ds(b, 1), :] + d[:, :npt] + d[:, npt:]
        return carry

    lax.fori_loop(0, nbat, one_batch, 0)


def potential_kernel(flag_ref, d_ref, ct_ref, v_ref, v2_ref, o_ref, hi_s, lo_s, *, first):
    nbat, kloc, _, _ = v_ref.shape
    slabs, rows, cap, _ = o_ref.shape
    group = kloc * SUB

    def one_batch(b, carry):
        d = d_ref[pl.ds(b, 1), :]
        pot = d / jnp.sqrt(1.0 + d * d)
        pot = jnp.concatenate([pot, pot], axis=1)
        left = v2_ref[b, first * SUB : (first + rows) * SUB].astype(F32)
        g = dot_nt((left * pot).astype(BF16), diagonal_values(v_ref, b))
        at = pl.ds(pl.multiple_of(b * group, group), group)
        for j in range(rows):
            x = jnp.concatenate(
                [g[j * SUB : (j + 1) * SUB, l * LANES : (l + 1) * LANES] for l in range(kloc)],
                axis=0,
            )
            hi, lo = split_pair(x)
            hi_s[j, at, :] = hi
            lo_s[j, at, :] = lo
        return carry

    lax.fori_loop(0, nbat, one_batch, 0)

    def sums(jp, parts):
        hi = jnp.concatenate([hi_s[2 * jp], hi_s[2 * jp + 1]], axis=1)
        lo = jnp.concatenate([lo_s[2 * jp], lo_s[2 * jp + 1]], axis=1)
        lhs = [ct_ref[n] for n in range(parts) for _ in range(2)]
        out = dot_nn(jnp.concatenate(lhs, axis=1), jnp.concatenate([hi, lo] * parts, axis=0))
        out = out.astype(BF16)
        o_ref[:, 2 * jp] = out[:, :LANES].reshape(slabs, cap, LANES)
        o_ref[:, 2 * jp + 1] = out[:, LANES:].reshape(slabs, cap, LANES)

    def loop(parts, unroll):
        def step(jp, carry):
            sums(jp, parts)
            return carry

        lax.fori_loop(0, rows // 2, step, 0, unroll=unroll)

    @pl.when(flag_ref[0, 0] == 0)
    def _():
        loop(1, 2)

    @pl.when(flag_ref[0, 0] != 0)
    def _():
        loop(2, 1)


def owner_sums(hot_ref, ret_ref):
    hot = hot_ref[...]
    parts = []
    for jp in range(ret_ref.shape[1] // 2):
        res = dot_tn(hot, slot_rows(ret_ref, jp))
        parts += [res[:, :LANES], res[:, LANES:]]
    return jnp.swapaxes(jnp.stack(parts, axis=0), 0, 1)


def owner_kernel(hot_ref, ret_ref, old_ref, o_ref, buf, sem, *, first):
    bs = o_ref.shape[2]
    half = o_ref.shape[1] // 2
    rows = ret_ref.shape[1]
    sums = owner_sums(hot_ref, ret_ref)
    copies = []
    for h in range(2):
        buf[h] = sums[:, :, h * bs : (h + 1) * bs]
        copies.append(
            pltpu.make_async_copy(
                buf.at[h], o_ref.at[:, pl.ds(h * half + first, rows)], sem.at[h]
            )
        )
        copies[-1].start()
    for c in copies:
        c.wait()


SMEM = pl.BlockSpec(memory_space=pltpu.SMEM)
VMEM = pl.BlockSpec(memory_space=pltpu.VMEM)
ANY = pl.BlockSpec(memory_space=pl.ANY)
PARAMS = pltpu.CompilerParams(vmem_limit_bytes=32 << 20)


def exchange(x):
    x = lax.all_to_all(x, "slab", split_axis=0, concat_axis=0, tiled=True)
    return x


def body(p_blocks, basis_vals, need_list, tasks, task_counts):
    own = p_blocks[0]
    blk_dev, bs, _ = own.shape
    nbat, kloc, _, npt = basis_vals.shape
    slabs, cap = need_list.shape[2:]
    slots = slabs * cap
    half = bs // 2
    rows = half // PARTS
    keys = nbat * kloc * kloc
    wide = jax.ShapeDtypeStruct((slabs, rows, cap, LANES), BF16)

    requested = exchange(need_list.reshape(slabs, 1, cap))

    own_rows = pl.pallas_call(
        own_kernel,
        out_shape=jax.ShapeDtypeStruct((half // 2, blk_dev, 2 * LANES), BF16),
        in_specs=[VMEM],
        out_specs=VMEM,
        compiler_params=PARAMS,
        name="own",
    )(own)

    counts, counts_t, v2, flag = pl.pallas_call(
        prep_kernel,
        out_shape=(
            jax.ShapeDtypeStruct((2, keys, slots), BF16),
            jax.ShapeDtypeStruct((2, slots, keys), BF16),
            jax.ShapeDtypeStruct((nbat, half * kloc, 2 * npt), BF16),
            jax.ShapeDtypeStruct((1, 1), jnp.int32),
        ),
        in_specs=[SMEM, VMEM, VMEM],
        out_specs=(VMEM, VMEM, VMEM, SMEM),
        compiler_params=PARAMS,
        name="prep",
    )(task_counts, tasks[0, 0], basis_vals)

    sent, hot = pl.pallas_call(
        first_send_kernel,
        out_shape=(wide, jax.ShapeDtypeStruct((slots, blk_dev), BF16)),
        in_specs=[VMEM, VMEM],
        out_specs=(VMEM, VMEM),
        compiler_params=PARAMS,
        name="send0",
    )(requested, own_rows)
    received = [exchange(sent)]
    for n in range(1, PARTS):
        sent = pl.pallas_call(
            functools.partial(next_send_kernel, first=n * rows),
            out_shape=wide,
            in_specs=[VMEM, VMEM],
            out_specs=VMEM,
            compiler_params=PARAMS,
            name=f"send{n}",
        )(hot, own_rows)
        received.append(exchange(sent))

    partial = jnp.zeros((nbat, npt), F32)
    for n in range(PARTS):
        partial = pl.pallas_call(
            functools.partial(density_kernel, first=n * rows),
            out_shape=jax.ShapeDtypeStruct((nbat, npt), F32),
            in_specs=[SMEM] + [VMEM] * 5,
            out_specs=VMEM,
            scratch_shapes=[pltpu.VMEM((nbat * kloc, rows * SUB, LANES), BF16)] * 2,
            compiler_params=PARAMS,
            name=f"density{n}",
        )(flag, received[n], counts, basis_vals, v2, partial)
    density = lax.psum(partial, "blk")

    returned = []
    for n in range(PARTS):
        slot_sums = pl.pallas_call(
            functools.partial(potential_kernel, first=n * rows),
            out_shape=wide,
            in_specs=[SMEM] + [VMEM] * 4,
            out_specs=VMEM,
            scratch_shapes=[pltpu.VMEM((rows, keys, LANES), BF16)] * 2,
            compiler_params=PARAMS,
            name=f"potential{n}",
        )(flag, density, counts_t, basis_vals, v2)
        returned.append(exchange(slot_sums))

    out = pl.empty((blk_dev, bs, bs), F32) if False else None
    out_shape = jax.ShapeDtypeStruct((blk_dev, bs, bs), F32)
    for n in range(PARTS):
        args = (hot, returned[n]) + (() if out is None else (out,))
        kern = functools.partial(owner_kernel, first=n * rows)
        if out is None:
            kern = functools.partial(
                lambda h, r, o, b, s, first: owner_kernel(h, r, None, o, b, s, first=first),
                first=n * rows,
            )
        out = pl.pallas_call(
            kern,
            out_shape=out_shape,
            in_specs=[VMEM, VMEM] + [ANY] * (len(args) - 2),
            out_specs=ANY,
            scratch_shapes=[
                pltpu.VMEM((2, blk_dev, rows, bs), F32),
                pltpu.SemaphoreType.DMA((2,)),
            ],
            input_output_aliases={2: 0} if len(args) == 3 else {},
            compiler_params=PARAMS,
            name=f"owner{n}",
        )(*args)
    return (density, out[None])


def solution(mesh):
    in_specs = (
        P("blk", "slab", None, None),
        P("slab", None, None, None),
        P("blk", "slab", None, None),
        P("blk", "slab", None, None),
        P("blk", "slab"),
    )
    out_specs = (P("slab", None), P("blk", "slab", None, None))
    return jax.shard_map(body, mesh=mesh, in_specs=in_specs, out_specs=out_specs, check_vma=False)
```

```python
import jax
import jax.numpy as jnp
from jax import lax
from jax.experimental import pallas as pl
from jax.experimental.pallas import tpu as pltpu
from jax.sharding import PartitionSpec as P

F32 = jnp.float32
BF16 = jnp.bfloat16
LANES = 128
SUB = 8
TASK_STEP = 512


def dot_nn(a, b):
    return lax.dot_general(a, b, (((1,), (0,)), ((), ())), preferred_element_type=F32)


def dot_nt(a, b):
    return lax.dot_general(a, b, (((1,), (1,)), ((), ())), preferred_element_type=F32)


def split_pair(x):
    hi = x.astype(BF16)
    return hi, (x - hi.astype(F32)).astype(BF16)


def turn_kernel(x_ref, o_ref):
    x = jnp.transpose(x_ref[...])
    o_ref[...] = x.reshape(o_ref.shape)


def own_kernel(own_ref, o_ref):
    half = own_ref.shape[1] // 2
    own = own_ref[...].astype(F32)
    own = jnp.concatenate([own[:, :half], own[:, half:]], axis=2)
    own = jnp.swapaxes(own, 0, 1).astype(BF16)
    for j in range(half):
        o_ref[j // 2, :, (j % 2) * LANES : (j % 2 + 1) * LANES] = own[j]


def prep_kernel(
    count_ref, tasks_ref, v_ref, hot_ref, c_ref, ct_ref, v2_ref, hot_t_ref, flag_ref
):
    hot_t_ref[...] = jnp.transpose(hot_ref[...].astype(F32)).astype(BF16)
    nbat, kloc, bs, npt = v_ref.shape
    keys = nbat * kloc * kloc
    slots = c_ref.shape[2]
    tcap = tasks_ref.shape[1]
    step = TASK_STEP if tcap % TASK_STEP == 0 else tcap
    live = count_ref[0, 0]
    c = jnp.zeros((keys, slots), F32)
    ct = jnp.zeros((slots, keys), F32)
    for t in range(0, tcap, step):
        fields = tasks_ref[:, t : t + step]
        key = (fields[0:1] * kloc + fields[2:3]) * kloc + fields[1:2]
        lane = lax.broadcasted_iota(jnp.int32, (1, step), 1) + t
        key = jnp.where(lane < live, key, -1)
        key_hot = jnp.where(
            lax.broadcasted_iota(jnp.int32, (keys, step), 0) == key, 1.0, 0.0
        ).astype(BF16)
        slot_hot = jnp.where(
            lax.broadcasted_iota(jnp.int32, (slots, step), 0) == fields[3:4], 1.0, 0.0
        ).astype(BF16)
        c += dot_nt(key_hot, slot_hot)
        ct += dot_nt(slot_hot, key_hot)
    c_hi = jnp.floor(c * (1.0 / 256.0)) * 256.0
    ct_hi = jnp.floor(ct * (1.0 / 256.0)) * 256.0
    c_ref[0] = (c - c_hi).astype(BF16)
    c_ref[1] = c_hi.astype(BF16)
    ct_ref[0] = (ct - ct_hi).astype(BF16)
    ct_ref[1] = ct_hi.astype(BF16)
    flag_ref[0, 0] = jnp.where(jnp.max(c) > 255.5, 1, 0).astype(jnp.int32)
    half = bs // 2
    for b in range(nbat):
        vals = jnp.swapaxes(v_ref[b].astype(F32), 0, 1)
        for h in range(2):
            part = vals[h * half : (h + 1) * half].reshape(half * kloc, npt)
            v2_ref[b, :, h * npt : (h + 1) * npt] = part.astype(BF16)


def request_hot(req_ref, nblk):
    slabs, _, cap = req_ref.shape
    slots = slabs * cap
    req = req_ref[...].reshape(slabs, cap).astype(F32).astype(BF16)
    row = lax.broadcasted_iota(jnp.int32, (slots, slabs), 0) // cap
    col = lax.broadcasted_iota(jnp.int32, (slots, slabs), 1)
    spread = dot_nn(jnp.where(row == col, 1.0, 0.0).astype(BF16), req)
    nth = lax.broadcasted_iota(jnp.int32, (slots, cap), 0) % cap
    keep = lax.broadcasted_iota(jnp.int32, (slots, cap), 1) == nth
    ids = jnp.sum(jnp.where(keep, spread, 0.0), axis=1, keepdims=True).astype(jnp.int32)
    ids = jnp.broadcast_to(ids, (slots, nblk))
    same = lax.broadcasted_iota(jnp.int32, (slots, nblk), 1) == ids
    return jnp.where(same, 1.0, 0.0).astype(BF16)


def send_kernel(req_ref, own_ref, o_ref, hot_ref, buf, sem):
    slabs, rows, cap, _ = buf.shape
    hot = request_hot(req_ref, own_ref.shape[1])
    hot_ref[...] = hot
    group = rows // sem.shape[0]
    copies = []
    for jp in range(rows // 2):
        res = dot_nn(hot, own_ref[jp]).astype(BF16)
        buf[:, 2 * jp] = res[:, :LANES].reshape(slabs, cap, LANES)
        buf[:, 2 * jp + 1] = res[:, LANES:].reshape(slabs, cap, LANES)
        if (2 * jp + 2) % group == 0:
            n = len(copies)
            part = pl.ds(n * group, group)
            copies.append(pltpu.make_async_copy(buf.at[:, part], o_ref.at[:, part], sem.at[n]))
            copies[n].start()
    for copy in copies:
        copy.wait()


def slot_rows(ref, jp):
    slabs, _, cap, _ = ref.shape
    r0 = ref[:, 2 * jp].reshape(slabs * cap, LANES)
    r1 = ref[:, 2 * jp + 1].reshape(slabs * cap, LANES)
    return jnp.concatenate([r0, r1], axis=1)


def diagonal_values(v_ref, b):
    _, kloc, bs, npt = v_ref.shape
    zero = jnp.zeros((bs, npt), BF16)
    rows = []
    for l in range(kloc):
        v = v_ref[b, l]
        rows.append(jnp.concatenate([v, zero], axis=1))
        rows.append(jnp.concatenate([zero, v], axis=1))
    return jnp.concatenate(rows, axis=0)


def density_kernel(
    flag_ref, r_ref, c_hbm, v_hbm, v2_hbm, d_ref, c_ref, v_ref, v2_ref, hi_s, lo_s, even, odd, sem
):
    nbat, kloc, _, npt = v_ref.shape
    rows = r_ref.shape[1]
    keys = c_ref.shape[1]
    get_c = pltpu.make_async_copy(c_hbm, c_ref, sem.at[0])
    get_v = pltpu.make_async_copy(v_hbm, v_ref, sem.at[1])
    get_v2 = pltpu.make_async_copy(v2_hbm, v2_ref, sem.at[2])
    get_c.start()
    get_v.start()
    get_v2.start()

    def build(jp, rhs_ref, parts):
        rhs = rhs_ref[...]
        res = dot_nn(c_ref[0], rhs)
        if parts == 2:
            res += dot_nn(c_ref[1], rhs)
        res = res.reshape(keys // SUB, SUB, 2 * LANES)
        hi, lo = split_pair(jnp.concatenate([res[:, :, :LANES], res[:, :, LANES:]], axis=1))
        at = pl.ds(pl.multiple_of(jp * 2 * SUB, 2 * SUB), 2 * SUB)
        hi_s[:, at, :] = hi
        lo_s[:, at, :] = lo

    even[...] = slot_rows(r_ref, 0)
    get_c.wait()

    def loop(parts):

        def step(i, carry):
            odd[...] = slot_rows(r_ref, 2 * i + 1)
            build(2 * i, even, parts)
            even[...] = slot_rows(r_ref, jnp.minimum(2 * i + 2, rows // 2 - 1))
            build(2 * i + 1, odd, parts)
            return carry

        lax.fori_loop(0, rows // 4, step, 0)

    @pl.when(flag_ref[0, 0] == 0)
    def _():
        loop(1)

    @pl.when(flag_ref[0, 0] != 0)
    def _():
        loop(2)

    get_v.wait()
    get_v2.wait()

    def one_batch(b, carry):
        lhs = jnp.concatenate(
            [
                jnp.concatenate([hi_s[b * kloc + l] for l in range(kloc)], axis=1),
                jnp.concatenate([lo_s[b * kloc + l] for l in range(kloc)], axis=1),
            ],
            axis=0,
        )
        image = dot_nn(lhs, diagonal_values(v_ref, b))
        image = image[: rows * SUB] + image[rows * SUB :]
        d = jnp.sum(image * v2_ref[b].astype(F32), axis=0, keepdims=True)
        d_ref[pl.ds(b, 1), :] = d[:, :npt] + d[:, npt:]
        return carry

    lax.fori_loop(0, nbat, one_batch, 0, unroll=2)


def potential_kernel(
    flag_ref, d_ref, ct_hbm, v_hbm, v2_hbm, o_ref, ct_ref, v_ref, v2_ref, hi_s, lo_s, pot_s, sem
):
    nbat, kloc, _, _ = v_ref.shape

    def get_batch(b):
        return (
            pltpu.make_async_copy(v_hbm.at[b], v_ref.at[b], sem.at[0, b]),
            pltpu.make_async_copy(v2_hbm.at[b], v2_ref.at[b], sem.at[1, b]),
        )

    get_ct = pltpu.make_async_copy(ct_hbm, ct_ref, sem.at[2, 0])
    for b in range(nbat):
        for copy in get_batch(b):
            copy.start()
    get_ct.start()
    slabs, rows, cap, _ = o_ref.shape
    group = kloc * SUB
    d = d_ref[...]
    pot = d / jnp.sqrt(1.0 + d * d)
    pot_s[...] = jnp.concatenate([pot, pot], axis=1)

    def one_batch(b, carry):
        for copy in get_batch(b):
            copy.wait()
        weighted = (v2_ref[b].astype(F32) * pot_s[pl.ds(b, 1), :]).astype(BF16)
        g = dot_nt(weighted, diagonal_values(v_ref, b))
        at = pl.ds(pl.multiple_of(b * group, group), group)
        for j in range(rows):
            x = jnp.concatenate(
                [g[j * SUB : (j + 1) * SUB, l * LANES : (l + 1) * LANES] for l in range(kloc)],
                axis=0,
            )
            hi, lo = split_pair(x)
            hi_s[j, at, :] = hi
            lo_s[j, at, :] = lo
        return carry

    lax.fori_loop(0, nbat, one_batch, 0, unroll=1)
    get_ct.wait()

    def sums(jp, parts):
        hi = jnp.concatenate([hi_s[2 * jp], hi_s[2 * jp + 1]], axis=1)
        lo = jnp.concatenate([lo_s[2 * jp], lo_s[2 * jp + 1]], axis=1)
        lhs = [ct_ref[n] for n in range(parts) for _ in range(2)]
        out = dot_nn(jnp.concatenate(lhs, axis=1), jnp.concatenate([hi, lo] * parts, axis=0))
        out = out.astype(BF16)
        o_ref[:, 2 * jp] = out[:, :LANES].reshape(slabs, cap, LANES)
        o_ref[:, 2 * jp + 1] = out[:, LANES:].reshape(slabs, cap, LANES)

    def loop(parts, unroll):
        def step(jp, carry):
            sums(jp, parts)
            return carry

        lax.fori_loop(0, rows // 2, step, 0, unroll=unroll)

    @pl.when(flag_ref[0, 0] == 0)
    def _():
        loop(1, 2)

    @pl.when(flag_ref[0, 0] != 0)
    def _():
        loop(2, 1)


def owner_kernel(hot_ref, ret_ref, o_ref):
    bs = o_ref.shape[2]
    half = o_ref.shape[1] // 2
    hot = hot_ref[...]
    parts = []
    for jp in range(half // 2):
        res = dot_nn(hot, slot_rows(ret_ref, jp))
        parts += [res[:, :LANES], res[:, LANES:]]
    sums = jnp.swapaxes(jnp.stack(parts, axis=0), 0, 1)
    o_ref[:, :half] = sums[:, :, :bs]
    o_ref[:, half:] = sums[:, :, bs:]


SMEM = pl.BlockSpec(memory_space=pltpu.SMEM)
VMEM = pl.BlockSpec(memory_space=pltpu.VMEM)
HBM = pl.BlockSpec(memory_space=pltpu.HBM)


def kernel_call(kernel, name, mib, **kwargs):
    params = pltpu.CompilerParams(vmem_limit_bytes=mib << 20)
    return pl.pallas_call(kernel, compiler_params=params, name=name, **kwargs)


def in_hbm(x):
    return pltpu.with_memory_space_constraint(x, pltpu.HBM)


def exchange(x):
    return lax.all_to_all(x, "slab", split_axis=0, concat_axis=0, tiled=True)


def body(p_blocks, basis_vals, need_list, tasks, task_counts):
    own = p_blocks[0]
    blk_dev, bs, _ = own.shape
    nbat, kloc, _, npt = basis_vals.shape
    slabs, cap = need_list.shape[2:]
    slots = slabs * cap
    half = bs // 2
    keys = nbat * kloc * kloc
    wide = jax.ShapeDtypeStruct((slabs, half, cap, LANES), BF16)

    wanted = kernel_call(
        turn_kernel,
        "turn",
        4,
        out_shape=jax.ShapeDtypeStruct((slabs, 1, cap), jnp.int32),
        in_specs=[VMEM],
        out_specs=VMEM,
    )(need_list[0, 0].T)
    requested = exchange(wanted)

    own_rows = kernel_call(
        own_kernel,
        "own",
        8,
        out_shape=jax.ShapeDtypeStruct((half // 2, blk_dev, 2 * LANES), BF16),
        in_specs=[VMEM],
        out_specs=VMEM,
    )(own)

    sent, hot = kernel_call(
        send_kernel,
        "send",
        8,
        out_shape=(pltpu.HBM(wide.shape, BF16), jax.ShapeDtypeStruct((slots, blk_dev), BF16)),
        in_specs=[VMEM, VMEM],
        out_specs=(HBM, VMEM),
        scratch_shapes=[pltpu.VMEM(wide.shape, BF16), pltpu.SemaphoreType.DMA((4,))],
    )(requested, own_rows)
    received = exchange(sent)

    counts, counts_t, v2, hot_t, flag = kernel_call(
        prep_kernel,
        "prep",
        16,
        out_shape=(
            jax.ShapeDtypeStruct((2, keys, slots), BF16),
            jax.ShapeDtypeStruct((2, slots, keys), BF16),
            jax.ShapeDtypeStruct((nbat, half * kloc, 2 * npt), BF16),
            jax.ShapeDtypeStruct((blk_dev, slots), BF16),
            jax.ShapeDtypeStruct((1, 1), jnp.int32),
        ),
        in_specs=[SMEM, VMEM, VMEM, VMEM],
        out_specs=(VMEM, VMEM, VMEM, VMEM, SMEM),
    )(task_counts, tasks[0, 0], basis_vals, hot)

    partial = kernel_call(
        density_kernel,
        "density",
        16,
        out_shape=jax.ShapeDtypeStruct((nbat, npt), F32),
        in_specs=[SMEM, VMEM, HBM, HBM, HBM],
        out_specs=VMEM,
        scratch_shapes=[
            pltpu.VMEM(counts.shape, BF16),
            pltpu.VMEM(basis_vals.shape, BF16),
            pltpu.VMEM(v2.shape, BF16),
        ]
        + [pltpu.VMEM((nbat * kloc, half * SUB, LANES), BF16)] * 2
        + [pltpu.VMEM((slots, 2 * LANES), BF16)] * 2
        + [pltpu.SemaphoreType.DMA((3,))],
    )(flag, received, in_hbm(counts), in_hbm(basis_vals), in_hbm(v2))
    density = lax.psum(partial, "blk")

    slot_sums = kernel_call(
        potential_kernel,
        "potential",
        16,
        out_shape=wide,
        in_specs=[SMEM, VMEM, HBM, HBM, HBM],
        out_specs=VMEM,
        scratch_shapes=[
            pltpu.VMEM(counts_t.shape, BF16),
            pltpu.VMEM(basis_vals.shape, BF16),
            pltpu.VMEM(v2.shape, BF16),
        ]
        + [pltpu.VMEM((half, keys, LANES), BF16)] * 2
        + [pltpu.VMEM((nbat, 2 * npt), F32), pltpu.SemaphoreType.DMA((3, nbat))],
    )(flag, density, in_hbm(counts_t), in_hbm(basis_vals), in_hbm(v2))
    returned = exchange(slot_sums)

    owner_sums = kernel_call(
        owner_kernel,
        "owner",
        8,
        out_shape=jax.ShapeDtypeStruct((blk_dev, bs, bs), F32),
        in_specs=[VMEM, VMEM],
        out_specs=VMEM,
    )(hot_t, returned)
    return (density, owner_sums[None])


def solution(mesh):
    in_specs = (
        P("blk", "slab", None, None),
        P("slab", None, None, None),
        P("blk", "slab", None, None),
        P("blk", "slab", None, None),
        P("blk", "slab"),
    )
    out_specs = (P("slab", None), P("blk", "slab", None, None))
    return jax.shard_map(body, mesh=mesh, in_specs=in_specs, out_specs=out_specs, check_vma=False)
```

```python
import jax
import jax.numpy as jnp
from jax import lax
from jax.experimental import pallas as pl
from jax.experimental.pallas import tpu as pltpu
from jax.sharding import PartitionSpec as P

F32 = jnp.float32
BF16 = jnp.bfloat16
LANES = 128
SUB = 8
TASK_STEP = 512
GROUP = 4
BATCH_GROUP = 4


def dot_nn(a, b):
    return lax.dot_general(a, b, (((1,), (0,)), ((), ())), preferred_element_type=F32)


def dot_nt(a, b):
    return lax.dot_general(a, b, (((1,), (1,)), ((), ())), preferred_element_type=F32)


def split_pair(x):
    hi = x.astype(BF16)
    return hi, (x - hi.astype(F32)).astype(BF16)


def turn_kernel(x_ref, o_ref):
    x = jnp.transpose(x_ref[...])
    o_ref[...] = x.reshape(o_ref.shape)


def own_kernel(own_ref, o_ref):
    half = own_ref.shape[1] // 2
    own = own_ref[...].astype(F32)
    own = jnp.concatenate([own[:, :half], own[:, half:]], axis=2)
    own = jnp.swapaxes(own, 0, 1).astype(BF16)
    for j in range(half):
        o_ref[j // 2, :, (j % 2) * LANES : (j % 2 + 1) * LANES] = own[j]


def prep_kernel(
    count_ref, tasks_ref, v_ref, hot_ref, c_ref, ct_ref, v2_ref, vt_ref, hot_t_ref, flag_ref
):
    hot_t_ref[...] = jnp.transpose(hot_ref[...].astype(F32)).astype(BF16)
    nbat, kloc, bs, npt = v_ref.shape
    keys = nbat * kloc * kloc
    slots = c_ref.shape[2]
    tcap = tasks_ref.shape[1]
    step = TASK_STEP if tcap % TASK_STEP == 0 else tcap
    live = count_ref[0, 0]
    c = jnp.zeros((keys, slots), F32)
    ct = jnp.zeros((slots, keys), F32)
    for t in range(0, tcap, step):
        fields = tasks_ref[:, t : t + step]
        key = (fields[0:1] * kloc + fields[2:3]) * kloc + fields[1:2]
        lane = lax.broadcasted_iota(jnp.int32, (1, step), 1) + t
        key = jnp.where(lane < live, key, -1)
        key_hot = jnp.where(
            lax.broadcasted_iota(jnp.int32, (keys, step), 0) == key, 1.0, 0.0
        ).astype(BF16)
        slot_hot = jnp.where(
            lax.broadcasted_iota(jnp.int32, (slots, step), 0) == fields[3:4], 1.0, 0.0
        ).astype(BF16)
        c += dot_nt(key_hot, slot_hot)
        ct += dot_nt(slot_hot, key_hot)
    c_hi = jnp.floor(c * (1.0 / 256.0)) * 256.0
    ct_hi = jnp.floor(ct * (1.0 / 256.0)) * 256.0
    c_ref[0] = (c - c_hi).astype(BF16)
    c_ref[1] = c_hi.astype(BF16)
    ct_ref[0] = (ct - ct_hi).astype(BF16)
    ct_ref[1] = ct_hi.astype(BF16)
    flag_ref[0, 0] = jnp.where(jnp.max(c) > 255.5, 1, 0).astype(jnp.int32)
    half = bs // 2
    for b in range(nbat):
        vals = jnp.swapaxes(v_ref[b].astype(F32), 0, 1)
        for h in range(2):
            part = vals[h * half : (h + 1) * half].reshape(half * kloc, npt)
            v2_ref[b, :, h * npt : (h + 1) * npt] = part.astype(BF16)
        zero = jnp.zeros((npt, bs), F32)
        for l in range(kloc):
            vt = jnp.transpose(v_ref[b, l].astype(F32))
            vt_ref[b, l, :npt] = jnp.concatenate([vt, zero], axis=1).astype(BF16)
            vt_ref[b, l, npt:] = jnp.concatenate([zero, vt], axis=1).astype(BF16)


def request_hot(req_ref, nblk):
    slabs, _, cap = req_ref.shape
    slots = slabs * cap
    req = req_ref[...].reshape(slabs, cap).astype(F32).astype(BF16)
    row = lax.broadcasted_iota(jnp.int32, (slots, slabs), 0) // cap
    col = lax.broadcasted_iota(jnp.int32, (slots, slabs), 1)
    spread = dot_nn(jnp.where(row == col, 1.0, 0.0).astype(BF16), req)
    nth = lax.broadcasted_iota(jnp.int32, (slots, cap), 0) % cap
    keep = lax.broadcasted_iota(jnp.int32, (slots, cap), 1) == nth
    ids = jnp.sum(jnp.where(keep, spread, 0.0), axis=1, keepdims=True).astype(jnp.int32)
    ids = jnp.broadcast_to(ids, (slots, nblk))
    same = lax.broadcasted_iota(jnp.int32, (slots, nblk), 1) == ids
    return jnp.where(same, 1.0, 0.0).astype(BF16)


def send_kernel(req_ref, own_ref, o_ref, hot_ref, buf, sem):
    slabs, rows, cap, _ = buf.shape
    hot = request_hot(req_ref, own_ref.shape[1])
    hot_ref[...] = hot
    group = rows // sem.shape[0]
    copies = []
    for jp in range(rows // 2):
        res = dot_nn(hot, own_ref[jp]).astype(BF16)
        buf[:, 2 * jp] = res[:, :LANES].reshape(slabs, cap, LANES)
        buf[:, 2 * jp + 1] = res[:, LANES:].reshape(slabs, cap, LANES)
        if (2 * jp + 2) % group == 0:
            n = len(copies)
            part = pl.ds(n * group, group)
            copies.append(pltpu.make_async_copy(buf.at[:, part], o_ref.at[:, part], sem.at[n]))
            copies[n].start()
    for copy in copies:
        copy.wait()


def slot_rows(ref, jp):
    slabs, _, cap, _ = ref.shape
    r0 = ref[:, 2 * jp].reshape(slabs * cap, LANES)
    r1 = ref[:, 2 * jp + 1].reshape(slabs * cap, LANES)
    return jnp.concatenate([r0, r1], axis=1)


def diagonal_values(v_ref, b):
    _, kloc, bs, npt = v_ref.shape
    zero = jnp.zeros((bs, npt), BF16)
    rows = []
    for l in range(kloc):
        v = v_ref[b, l]
        rows.append(jnp.concatenate([v, zero], axis=1))
        rows.append(jnp.concatenate([zero, v], axis=1))
    return jnp.concatenate(rows, axis=0)


def density_kernel(
    flag_ref, r_ref, c_hbm, v_hbm, v2_hbm, d_ref, c_ref, v_ref, v2_ref, hi_s, lo_s, sem
):
    nbat, kloc, _, npt = v_ref.shape
    rows = r_ref.shape[1]
    keys = c_ref.shape[1]
    get_c = pltpu.make_async_copy(c_hbm, c_ref, sem.at[0])
    get_v = pltpu.make_async_copy(v_hbm, v_ref, sem.at[1])
    get_v2 = pltpu.make_async_copy(v2_hbm, v2_ref, sem.at[2])
    get_c.start()
    get_v.start()
    get_v2.start()

    def build(jp, parts):
        rhs = slot_rows(r_ref, jp)
        res = dot_nn(c_ref[0], rhs)
        if parts == 2:
            res += dot_nn(c_ref[1], rhs)
        res = res.reshape(keys // SUB, SUB, 2 * LANES)
        hi, lo = split_pair(jnp.concatenate([res[:, :, :LANES], res[:, :, LANES:]], axis=1))
        at = pl.ds(pl.multiple_of(jp * 2 * SUB, 2 * SUB), 2 * SUB)
        hi_s[:, at, :] = hi
        lo_s[:, at, :] = lo

    get_c.wait()

    def loop(parts, group):
        def step(i, carry):
            for n in range(group):
                build(group * i + n, parts)
            return carry

        lax.fori_loop(0, rows // (2 * group), step, 0)

    @pl.when(flag_ref[0, 0] == 0)
    def _():
        loop(1, GROUP)

    @pl.when(flag_ref[0, 0] != 0)
    def _():
        loop(2, 1)

    get_v.wait()
    get_v2.wait()

    def one_batch(b, carry):
        lhs = jnp.concatenate(
            [
                jnp.concatenate([hi_s[b * kloc + l] for l in range(kloc)], axis=1),
                jnp.concatenate([lo_s[b * kloc + l] for l in range(kloc)], axis=1),
            ],
            axis=0,
        )
        image = dot_nn(lhs, diagonal_values(v_ref, b))
        image = image[: rows * SUB] + image[rows * SUB :]
        d = jnp.sum(image * v2_ref[b].astype(F32), axis=0, keepdims=True)
        d_ref[pl.ds(b, 1), :] = d[:, :npt] + d[:, npt:]
        return carry

    lax.fori_loop(0, nbat, one_batch, 0, unroll=4)


def potential_kernel(
    flag_ref, d_ref, ct_hbm, vt_hbm, v2_hbm, o_ref, ct_ref, vt_ref, v2_ref, g_s, pot_s, sem
):
    nbat, kloc, _, _ = vt_ref.shape
    slabs, rows, cap, _ = o_ref.shape

    def get_batch(b):
        return (
            pltpu.make_async_copy(vt_hbm.at[b], vt_ref.at[b], sem.at[0, b]),
            pltpu.make_async_copy(v2_hbm.at[b], v2_ref.at[b], sem.at[1, b]),
        )

    get_ct = pltpu.make_async_copy(ct_hbm, ct_ref, sem.at[2, 0])
    for b in range(nbat):
        for copy in get_batch(b):
            copy.start()
    get_ct.start()
    d = d_ref[...]
    pot = d / jnp.sqrt(1.0 + d * d)
    pot_s[...] = jnp.concatenate([pot, pot], axis=1)

    def one_batch(b):
        weighted = (v2_ref[b].astype(F32) * pot_s[pl.ds(b, 1), :]).astype(BF16)
        for lp in range(kloc // 2):
            rhs = jnp.concatenate([vt_ref[b, 2 * lp], vt_ref[b, 2 * lp + 1]], axis=1)
            g = dot_nn(weighted, rhs).reshape(rows, SUB, 2 * LANES)
            g = jnp.concatenate([g[:, :, :LANES], g[:, :, LANES:]], axis=1)
            row = pl.multiple_of((b * kloc + 2 * lp) * SUB, 2 * SUB)
            g_s[:, pl.ds(row, 2 * SUB), :] = g.astype(BF16)

    def some_batches(i, carry):
        for n in range(BATCH_GROUP):
            for copy in get_batch(i * BATCH_GROUP + n):
                copy.wait()
        for n in range(BATCH_GROUP):
            one_batch(i * BATCH_GROUP + n)
        return carry

    lax.fori_loop(0, nbat // BATCH_GROUP, some_batches, 0)
    get_ct.wait()

    def sums(jp, parts):
        rhs = jnp.concatenate([g_s[2 * jp], g_s[2 * jp + 1]], axis=1)
        out = dot_nn(ct_ref[0], rhs)
        if parts == 2:
            out += dot_nn(ct_ref[1], rhs)
        out = out.astype(BF16)
        o_ref[:, 2 * jp] = out[:, :LANES].reshape(slabs, cap, LANES)
        o_ref[:, 2 * jp + 1] = out[:, LANES:].reshape(slabs, cap, LANES)

    def loop(parts, group):
        def step(i, carry):
            for n in range(group):
                sums(group * i + n, parts)
            return carry

        lax.fori_loop(0, rows // (2 * group), step, 0)

    @pl.when(flag_ref[0, 0] == 0)
    def _():
        loop(1, 8)

    @pl.when(flag_ref[0, 0] != 0)
    def _():
        loop(2, 1)


def owner_kernel(hot_ref, ret_ref, o_ref):
    bs = o_ref.shape[2]
    half = o_ref.shape[1] // 2
    hot = hot_ref[...]
    parts = []
    for jp in range(half // 2):
        res = dot_nn(hot, slot_rows(ret_ref, jp))
        parts += [res[:, :LANES], res[:, LANES:]]
    sums = jnp.swapaxes(jnp.stack(parts, axis=0), 0, 1)
    o_ref[:, :half] = sums[:, :, :bs]
    o_ref[:, half:] = sums[:, :, bs:]


SMEM = pl.BlockSpec(memory_space=pltpu.SMEM)
VMEM = pl.BlockSpec(memory_space=pltpu.VMEM)
HBM = pl.BlockSpec(memory_space=pltpu.HBM)


def kernel_call(kernel, name, mib, **kwargs):
    params = pltpu.CompilerParams(vmem_limit_bytes=mib << 20)
    return pl.pallas_call(kernel, compiler_params=params, name=name, **kwargs)


def in_hbm(x):
    return pltpu.with_memory_space_constraint(x, pltpu.HBM)


def exchange(x):
    return lax.all_to_all(x, "slab", split_axis=0, concat_axis=0, tiled=True)


def body(p_blocks, basis_vals, need_list, tasks, task_counts):
    own = p_blocks[0]
    blk_dev, bs, _ = own.shape
    nbat, kloc, _, npt = basis_vals.shape
    slabs, cap = need_list.shape[2:]
    slots = slabs * cap
    half = bs // 2
    keys = nbat * kloc * kloc
    wide = jax.ShapeDtypeStruct((slabs, half, cap, LANES), BF16)

    wanted = kernel_call(
        turn_kernel,
        "turn",
        4,
        out_shape=jax.ShapeDtypeStruct((slabs, 1, cap), jnp.int32),
        in_specs=[VMEM],
        out_specs=VMEM,
    )(need_list[0, 0].T)
    requested = exchange(wanted)

    own_rows = kernel_call(
        own_kernel,
        "own",
        8,
        out_shape=jax.ShapeDtypeStruct((half // 2, blk_dev, 2 * LANES), BF16),
        in_specs=[VMEM],
        out_specs=VMEM,
    )(own)

    sent, hot = kernel_call(
        send_kernel,
        "send",
        8,
        out_shape=(pltpu.HBM(wide.shape, BF16), jax.ShapeDtypeStruct((slots, blk_dev), BF16)),
        in_specs=[VMEM, VMEM],
        out_specs=(HBM, VMEM),
        scratch_shapes=[pltpu.VMEM(wide.shape, BF16), pltpu.SemaphoreType.DMA((4,))],
    )(requested, own_rows)
    received = exchange(sent)

    counts, counts_t, v2, vt, hot_t, flag = kernel_call(
        prep_kernel,
        "prep",
        24,
        out_shape=(
            jax.ShapeDtypeStruct((2, keys, slots), BF16),
            jax.ShapeDtypeStruct((2, slots, keys), BF16),
            jax.ShapeDtypeStruct((nbat, half * kloc, 2 * npt), BF16),
            jax.ShapeDtypeStruct((nbat, kloc, 2 * npt, LANES), BF16),
            jax.ShapeDtypeStruct((blk_dev, slots), BF16),
            jax.ShapeDtypeStruct((1, 1), jnp.int32),
        ),
        in_specs=[SMEM, VMEM, VMEM, VMEM],
        out_specs=(VMEM, VMEM, VMEM, VMEM, VMEM, SMEM),
    )(task_counts, tasks[0, 0], basis_vals, hot)

    partial = kernel_call(
        density_kernel,
        "density",
        16,
        out_shape=jax.ShapeDtypeStruct((nbat, npt), F32),
        in_specs=[SMEM, VMEM, HBM, HBM, HBM],
        out_specs=VMEM,
        scratch_shapes=[
            pltpu.VMEM(counts.shape, BF16),
            pltpu.VMEM(basis_vals.shape, BF16),
            pltpu.VMEM(v2.shape, BF16),
        ]
        + [pltpu.VMEM((nbat * kloc, half * SUB, LANES), BF16)] * 2
        + [pltpu.SemaphoreType.DMA((3,))],
    )(flag, received, in_hbm(counts), in_hbm(basis_vals), in_hbm(v2))
    density = lax.psum(partial, "blk")

    slot_sums = kernel_call(
        potential_kernel,
        "potential",
        24,
        out_shape=wide,
        in_specs=[SMEM, VMEM, HBM, HBM, HBM],
        out_specs=VMEM,
        scratch_shapes=[
            pltpu.VMEM(counts_t.shape, BF16),
            pltpu.VMEM(vt.shape, BF16),
            pltpu.VMEM(v2.shape, BF16),
            pltpu.VMEM((half, keys, LANES), BF16),
            pltpu.VMEM((nbat, 2 * npt), F32),
            pltpu.SemaphoreType.DMA((3, nbat)),
        ],
    )(flag, density, in_hbm(counts_t), in_hbm(vt), in_hbm(v2))
    returned = exchange(slot_sums)

    owner_sums = kernel_call(
        owner_kernel,
        "owner",
        8,
        out_shape=jax.ShapeDtypeStruct((blk_dev, bs, bs), F32),
        in_specs=[VMEM, VMEM],
        out_specs=VMEM,
    )(hot_t, returned)
    return (density, owner_sums[None])


def solution(mesh):
    in_specs = (
        P("blk", "slab", None, None),
        P("slab", None, None, None),
        P("blk", "slab", None, None),
        P("blk", "slab", None, None),
        P("blk", "slab"),
    )
    out_specs = (P("slab", None), P("blk", "slab", None, None))
    return jax.shard_map(body, mesh=mesh, in_specs=in_specs, out_specs=out_specs, check_vma=False)
```

```python
import jax
import jax.numpy as jnp
from jax import lax
from jax.experimental import pallas as pl
from jax.experimental.pallas import tpu as pltpu
from jax.sharding import PartitionSpec as P

F32 = jnp.float32
BF16 = jnp.bfloat16
LANES = 128
SUB = 8
TASK_STEP = 512
GROUP = 4
BATCH_GROUP = 4


def dot_nn(a, b):
    return lax.dot_general(a, b, (((1,), (0,)), ((), ())), preferred_element_type=F32)


def dot_nt(a, b):
    return lax.dot_general(a, b, (((1,), (1,)), ((), ())), preferred_element_type=F32)


def split_pair(x):
    hi = x.astype(BF16)
    return hi, (x - hi.astype(F32)).astype(BF16)


def turn_kernel(x_ref, o_ref):
    x = jnp.transpose(x_ref[...])
    o_ref[...] = x.reshape(o_ref.shape)


def own_kernel(own_ref, o_ref):
    half = own_ref.shape[1] // 2
    own = own_ref[...].astype(F32)
    own = jnp.concatenate([own[:, :half], own[:, half:]], axis=2)
    own = jnp.swapaxes(own, 0, 1).astype(BF16)
    for j in range(half):
        o_ref[j // 2, :, (j % 2) * LANES : (j % 2 + 1) * LANES] = own[j]


def prep_kernel(
    count_ref, tasks_ref, v_ref, hot_ref, c_ref, ct_ref, v2_ref, vt_ref, hot_t_ref, flag_ref
):
    hot_t_ref[...] = jnp.transpose(hot_ref[...].astype(F32)).astype(BF16)
    nbat, kloc, bs, npt = v_ref.shape
    keys = nbat * kloc * kloc
    slots = c_ref.shape[2]
    tcap = tasks_ref.shape[1]
    step = TASK_STEP if tcap % TASK_STEP == 0 else tcap
    live = count_ref[0, 0]
    c = jnp.zeros((keys, slots), F32)
    ct = jnp.zeros((slots, keys), F32)
    for t in range(0, tcap, step):
        fields = tasks_ref[:, t : t + step]
        key = (fields[0:1] * kloc + fields[2:3]) * kloc + fields[1:2]
        lane = lax.broadcasted_iota(jnp.int32, (1, step), 1) + t
        key = jnp.where(lane < live, key, -1)
        key_hot = jnp.where(
            lax.broadcasted_iota(jnp.int32, (keys, step), 0) == key, 1.0, 0.0
        ).astype(BF16)
        slot_hot = jnp.where(
            lax.broadcasted_iota(jnp.int32, (slots, step), 0) == fields[3:4], 1.0, 0.0
        ).astype(BF16)
        c += dot_nt(key_hot, slot_hot)
        ct += dot_nt(slot_hot, key_hot)
    c_hi = jnp.floor(c * (1.0 / 256.0)) * 256.0
    ct_hi = jnp.floor(ct * (1.0 / 256.0)) * 256.0
    c_ref[0] = (c - c_hi).astype(BF16)
    c_ref[1] = c_hi.astype(BF16)
    ct_ref[0] = (ct - ct_hi).astype(BF16)
    ct_ref[1] = ct_hi.astype(BF16)
    flag_ref[0, 0] = jnp.where(jnp.max(c) > 255.5, 1, 0).astype(jnp.int32)
    half = bs // 2
    for b in range(nbat):
        vals = jnp.swapaxes(v_ref[b].astype(F32), 0, 1)
        for h in range(2):
            part = vals[h * half : (h + 1) * half].reshape(half * kloc, npt)
            v2_ref[b, :, h * npt : (h + 1) * npt] = part.astype(BF16)
        for l in range(kloc):
            vt = jnp.transpose(v_ref[b, l].astype(F32))
            vt_ref[b, l] = jnp.concatenate([vt, vt], axis=1).astype(BF16)


def request_hot(req_ref, nblk):
    slabs, _, cap = req_ref.shape
    slots = slabs * cap
    req = req_ref[...].reshape(slabs, cap).astype(F32).astype(BF16)
    row = lax.broadcasted_iota(jnp.int32, (slots, slabs), 0) // cap
    col = lax.broadcasted_iota(jnp.int32, (slots, slabs), 1)
    spread = dot_nn(jnp.where(row == col, 1.0, 0.0).astype(BF16), req)
    nth = lax.broadcasted_iota(jnp.int32, (slots, cap), 0) % cap
    keep = lax.broadcasted_iota(jnp.int32, (slots, cap), 1) == nth
    ids = jnp.sum(jnp.where(keep, spread, 0.0), axis=1, keepdims=True).astype(jnp.int32)
    ids = jnp.broadcast_to(ids, (slots, nblk))
    same = lax.broadcasted_iota(jnp.int32, (slots, nblk), 1) == ids
    return jnp.where(same, 1.0, 0.0).astype(BF16)


def send_kernel(req_ref, own_ref, o_ref, hot_ref, buf, sem):
    slabs, rows, cap, _ = buf.shape
    hot = request_hot(req_ref, own_ref.shape[1])
    hot_ref[...] = hot
    group = rows // sem.shape[0]
    copies = []
    for jp in range(rows // 2):
        res = dot_nn(hot, own_ref[jp]).astype(BF16)
        buf[:, 2 * jp] = res[:, :LANES].reshape(slabs, cap, LANES)
        buf[:, 2 * jp + 1] = res[:, LANES:].reshape(slabs, cap, LANES)
        if (2 * jp + 2) % group == 0:
            n = len(copies)
            part = pl.ds(n * group, group)
            copies.append(pltpu.make_async_copy(buf.at[:, part], o_ref.at[:, part], sem.at[n]))
            copies[n].start()
    for copy in copies:
        copy.wait()


def slot_rows(ref, jp):
    slabs, _, cap, _ = ref.shape
    r0 = ref[:, 2 * jp].reshape(slabs * cap, LANES)
    r1 = ref[:, 2 * jp + 1].reshape(slabs * cap, LANES)
    return jnp.concatenate([r0, r1], axis=1)


def diagonal_values(v_ref, b):
    _, kloc, bs, npt = v_ref.shape
    zero = jnp.zeros((bs, npt), BF16)
    rows = []
    for l in range(kloc):
        v = v_ref[b, l]
        rows.append(jnp.concatenate([v, zero], axis=1))
        rows.append(jnp.concatenate([zero, v], axis=1))
    return jnp.concatenate(rows, axis=0)


def density_kernel(
    flag_ref, r_ref, c_hbm, v_hbm, v2_hbm, d_ref, c_ref, v_ref, v2_ref, hi_s, lo_s, sem
):
    nbat, kloc, _, npt = v_ref.shape
    rows = r_ref.shape[1]
    keys = c_ref.shape[1]
    get_c = [pltpu.make_async_copy(c_hbm.at[n], c_ref.at[n], sem.at[n]) for n in range(2)]
    get_v = pltpu.make_async_copy(v_hbm, v_ref, sem.at[2])
    get_v2 = pltpu.make_async_copy(v2_hbm, v2_ref, sem.at[3])
    get_c[0].start()
    get_v.start()
    get_v2.start()
    get_c[1].start()

    def build(jp, parts):
        rhs = slot_rows(r_ref, jp)
        res = dot_nn(c_ref[0], rhs)
        if parts == 2:
            res += dot_nn(c_ref[1], rhs)
        res = res.reshape(keys // SUB, SUB, 2 * LANES)
        hi, lo = split_pair(jnp.concatenate([res[:, :, :LANES], res[:, :, LANES:]], axis=1))
        at = pl.ds(pl.multiple_of(jp * 2 * SUB, 2 * SUB), 2 * SUB)
        hi_s[:, at, :] = hi
        lo_s[:, at, :] = lo

    get_c[0].wait()

    def loop(parts, group):
        def step(i, carry):
            for n in range(group):
                build(group * i + n, parts)
            return carry

        lax.fori_loop(0, rows // (2 * group), step, 0)

    @pl.when(flag_ref[0, 0] == 0)
    def _():
        loop(1, 8)

    get_c[1].wait()

    @pl.when(flag_ref[0, 0] != 0)
    def _():
        loop(2, 1)

    get_v.wait()
    get_v2.wait()

    def one_batch(b, carry):
        lhs = jnp.concatenate(
            [
                jnp.concatenate([hi_s[b * kloc + l] for l in range(kloc)], axis=1),
                jnp.concatenate([lo_s[b * kloc + l] for l in range(kloc)], axis=1),
            ],
            axis=0,
        )
        image = dot_nn(lhs, diagonal_values(v_ref, b))
        image = image[: rows * SUB] + image[rows * SUB :]
        d = jnp.sum(image * v2_ref[b].astype(F32), axis=0, keepdims=True)
        d_ref[pl.ds(b, 1), :] = d[:, :npt] + d[:, npt:]
        return carry

    lax.fori_loop(0, nbat, one_batch, 0, unroll=4)


def potential_kernel(
    flag_ref,
    mine_ref,
    other_ref,
    ct_hbm,
    vt_hbm,
    v2_hbm,
    o_ref,
    d_ref,
    ct_ref,
    vt_ref,
    v2_ref,
    g_s,
    pot_s,
    sem,
):
    nbat, kloc, npt, _ = vt_ref.shape
    low = lax.broadcasted_iota(jnp.int32, (npt, LANES), 1) < LANES // 2
    slabs, rows, cap, _ = o_ref.shape

    def get_batch(b):
        return (
            pltpu.make_async_copy(vt_hbm.at[b], vt_ref.at[b], sem.at[0, b]),
            pltpu.make_async_copy(v2_hbm.at[b], v2_ref.at[b], sem.at[1, b]),
        )

    get_ct = pltpu.make_async_copy(ct_hbm, ct_ref, sem.at[2, 0])
    for b in range(nbat):
        for copy in get_batch(b):
            copy.start()
    get_ct.start()
    d = mine_ref[...] + other_ref[...]
    d_ref[...] = d
    pot = d / jnp.sqrt(1.0 + d * d)
    pot_s[...] = jnp.concatenate([pot, pot], axis=1)

    def one_batch(b):
        weighted = (v2_ref[b].astype(F32) * pot_s[pl.ds(b, 1), :]).astype(BF16)
        for lp in range(kloc // 2):
            pair = [vt_ref[b, 2 * lp], vt_ref[b, 2 * lp + 1]]
            zero = jnp.zeros_like(pair[0])
            top = jnp.concatenate([jnp.where(low, x, zero) for x in pair], axis=1)
            bottom = jnp.concatenate([jnp.where(low, zero, x) for x in pair], axis=1)
            rhs = jnp.concatenate([top, bottom], axis=0)
            g = dot_nn(weighted, rhs).reshape(rows, SUB, 2 * LANES)
            g = jnp.concatenate([g[:, :, :LANES], g[:, :, LANES:]], axis=1)
            row = pl.multiple_of((b * kloc + 2 * lp) * SUB, 2 * SUB)
            g_s[:, pl.ds(row, 2 * SUB), :] = g.astype(BF16)

    def some_batches(i, carry):
        for n in range(BATCH_GROUP):
            for copy in get_batch(i * BATCH_GROUP + n):
                copy.wait()
        for n in range(BATCH_GROUP):
            one_batch(i * BATCH_GROUP + n)
        return carry

    lax.fori_loop(0, nbat // BATCH_GROUP, some_batches, 0)
    get_ct.wait()

    def sums(jp, parts):
        rhs = jnp.concatenate([g_s[2 * jp], g_s[2 * jp + 1]], axis=1)
        out = dot_nn(ct_ref[0], rhs)
        if parts == 2:
            out += dot_nn(ct_ref[1], rhs)
        out = out.astype(BF16)
        o_ref[:, 2 * jp] = out[:, :LANES].reshape(slabs, cap, LANES)
        o_ref[:, 2 * jp + 1] = out[:, LANES:].reshape(slabs, cap, LANES)

    def loop(parts, group):
        def step(i, carry):
            for n in range(group):
                sums(group * i + n, parts)
            return carry

        lax.fori_loop(0, rows // (2 * group), step, 0)

    @pl.when(flag_ref[0, 0] == 0)
    def _():
        loop(1, 8)

    @pl.when(flag_ref[0, 0] != 0)
    def _():
        loop(2, 1)


def owner_kernel(hot_ref, ret_ref, o_ref):
    bs = o_ref.shape[2]
    half = o_ref.shape[1] // 2
    hot = hot_ref[...]
    parts = []
    for jp in range(half // 2):
        res = dot_nn(hot, slot_rows(ret_ref, jp))
        parts += [res[:, :LANES], res[:, LANES:]]
    sums = jnp.swapaxes(jnp.stack(parts, axis=0), 0, 1)
    o_ref[:, :half] = sums[:, :, :bs]
    o_ref[:, half:] = sums[:, :, bs:]


SMEM = pl.BlockSpec(memory_space=pltpu.SMEM)
VMEM = pl.BlockSpec(memory_space=pltpu.VMEM)
HBM = pl.BlockSpec(memory_space=pltpu.HBM)


def kernel_call(kernel, name, mib, **kwargs):
    params = pltpu.CompilerParams(vmem_limit_bytes=mib << 20)
    return pl.pallas_call(kernel, compiler_params=params, name=name, **kwargs)


def in_hbm(x):
    return pltpu.with_memory_space_constraint(x, pltpu.HBM)


def exchange(x):
    return lax.all_to_all(x, "slab", split_axis=0, concat_axis=0, tiled=True)


def body(p_blocks, basis_vals, need_list, tasks, task_counts):
    own = p_blocks[0]
    blk_dev, bs, _ = own.shape
    nbat, kloc, _, npt = basis_vals.shape
    slabs, cap = need_list.shape[2:]
    slots = slabs * cap
    half = bs // 2
    keys = nbat * kloc * kloc
    wide = jax.ShapeDtypeStruct((slabs, half, cap, LANES), BF16)

    wanted = kernel_call(
        turn_kernel,
        "turn",
        4,
        out_shape=jax.ShapeDtypeStruct((slabs, 1, cap), jnp.int32),
        in_specs=[VMEM],
        out_specs=VMEM,
    )(need_list[0, 0].T)
    requested = exchange(wanted)

    own_rows = kernel_call(
        own_kernel,
        "own",
        8,
        out_shape=jax.ShapeDtypeStruct((half // 2, blk_dev, 2 * LANES), BF16),
        in_specs=[VMEM],
        out_specs=VMEM,
    )(own)

    sent, hot = kernel_call(
        send_kernel,
        "send",
        8,
        out_shape=(pltpu.HBM(wide.shape, BF16), jax.ShapeDtypeStruct((slots, blk_dev), BF16)),
        in_specs=[VMEM, VMEM],
        out_specs=(HBM, VMEM),
        scratch_shapes=[pltpu.VMEM(wide.shape, BF16), pltpu.SemaphoreType.DMA((4,))],
    )(requested, own_rows)
    received = exchange(sent)

    counts, counts_t, v2, vt, hot_t, flag = kernel_call(
        prep_kernel,
        "prep",
        24,
        out_shape=(
            jax.ShapeDtypeStruct((2, keys, slots), BF16),
            jax.ShapeDtypeStruct((2, slots, keys), BF16),
            jax.ShapeDtypeStruct((nbat, half * kloc, 2 * npt), BF16),
            jax.ShapeDtypeStruct((nbat, kloc, npt, LANES), BF16),
            jax.ShapeDtypeStruct((blk_dev, slots), BF16),
            jax.ShapeDtypeStruct((1, 1), jnp.int32),
        ),
        in_specs=[SMEM, VMEM, VMEM, VMEM],
        out_specs=(VMEM, VMEM, VMEM, VMEM, VMEM, SMEM),
    )(task_counts, tasks[0, 0], basis_vals, hot)

    partial = kernel_call(
        density_kernel,
        "density",
        16,
        out_shape=jax.ShapeDtypeStruct((nbat, npt), F32),
        in_specs=[SMEM, VMEM, HBM, HBM, HBM],
        out_specs=VMEM,
        scratch_shapes=[
            pltpu.VMEM(counts.shape, BF16),
            pltpu.VMEM(basis_vals.shape, BF16),
            pltpu.VMEM(v2.shape, BF16),
        ]
        + [pltpu.VMEM((nbat * kloc, half * SUB, LANES), BF16)] * 2
        + [pltpu.SemaphoreType.DMA((4,))],
    )(flag, received, in_hbm(counts), in_hbm(basis_vals), in_hbm(v2))
    swap = [(0, 1), (1, 0)]
    other = lax.ppermute(partial, "blk", swap)

    slot_sums, density = kernel_call(
        potential_kernel,
        "potential",
        24,
        out_shape=(wide, jax.ShapeDtypeStruct((nbat, npt), F32)),
        in_specs=[SMEM, VMEM, VMEM, HBM, HBM, HBM],
        out_specs=(VMEM, VMEM),
        scratch_shapes=[
            pltpu.VMEM(counts_t.shape, BF16),
            pltpu.VMEM(vt.shape, BF16),
            pltpu.VMEM(v2.shape, BF16),
            pltpu.VMEM((half, keys, LANES), BF16),
            pltpu.VMEM((nbat, 2 * npt), F32),
            pltpu.SemaphoreType.DMA((3, nbat)),
        ],
    )(flag, partial, other, in_hbm(counts_t), in_hbm(vt), in_hbm(v2))
    returned = exchange(slot_sums)

    owner_sums = kernel_call(
        owner_kernel,
        "owner",
        8,
        out_shape=jax.ShapeDtypeStruct((blk_dev, bs, bs), F32),
        in_specs=[VMEM, VMEM],
        out_specs=VMEM,
    )(hot_t, returned)
    return (density, owner_sums[None])


def solution(mesh):
    in_specs = (
        P("blk", "slab", None, None),
        P("slab", None, None, None),
        P("blk", "slab", None, None),
        P("blk", "slab", None, None),
        P("blk", "slab"),
    )
    out_specs = (P("slab", None), P("blk", "slab", None, None))
    return jax.shard_map(body, mesh=mesh, in_specs=in_specs, out_specs=out_specs, check_vma=False)
```

```python
import jax
import jax.numpy as jnp
from jax import lax
from jax.experimental import pallas as pl
from jax.experimental.pallas import tpu as pltpu
from jax.sharding import PartitionSpec as P

F32 = jnp.float32
BF16 = jnp.bfloat16
LANES = 128
SUB = 8
TASK_STEP = 512
GROUP = 4
BATCH_GROUP = 4


def dot_nn(a, b):
    return lax.dot_general(a, b, (((1,), (0,)), ((), ())), preferred_element_type=F32)


def dot_nt(a, b):
    return lax.dot_general(a, b, (((1,), (1,)), ((), ())), preferred_element_type=F32)


def split_pair(x):
    hi = x.astype(BF16)
    return hi, (x - hi.astype(F32)).astype(BF16)


def turn_kernel(x_ref, o_ref):
    x = jnp.transpose(x_ref[...])
    o_ref[...] = x.reshape(o_ref.shape)


def own_kernel(own_ref, o_ref):
    half = own_ref.shape[1] // 2
    own = own_ref[...].astype(F32)
    own = jnp.concatenate([own[:, :half], own[:, half:]], axis=2)
    own = jnp.swapaxes(own, 0, 1).astype(BF16)
    for j in range(half):
        o_ref[j // 2, :, (j % 2) * LANES : (j % 2 + 1) * LANES] = own[j]


def prep_kernel(
    count_ref, tasks_ref, v_ref, hot_ref, c_ref, ct_ref, v2_ref, vt_ref, hot_t_ref, flag_ref
):
    hot_t_ref[...] = jnp.transpose(hot_ref[...].astype(F32)).astype(BF16)
    nbat, kloc, bs, npt = v_ref.shape
    keys = nbat * kloc * kloc
    slots = c_ref.shape[2]
    tcap = tasks_ref.shape[1]
    step = TASK_STEP if tcap % TASK_STEP == 0 else tcap
    live = count_ref[0, 0]
    c = jnp.zeros((keys, slots), F32)
    ct = jnp.zeros((slots, keys), F32)
    for t in range(0, tcap, step):
        fields = tasks_ref[:, t : t + step]
        key = (fields[0:1] * kloc + fields[2:3]) * kloc + fields[1:2]
        lane = lax.broadcasted_iota(jnp.int32, (1, step), 1) + t
        key = jnp.where(lane < live, key, -1)
        key_hot = jnp.where(
            lax.broadcasted_iota(jnp.int32, (keys, step), 0) == key, 1.0, 0.0
        ).astype(BF16)
        slot_hot = jnp.where(
            lax.broadcasted_iota(jnp.int32, (slots, step), 0) == fields[3:4], 1.0, 0.0
        ).astype(BF16)
        c += dot_nt(key_hot, slot_hot)
        ct += dot_nt(slot_hot, key_hot)
    c_hi = jnp.floor(c * (1.0 / 256.0)) * 256.0
    ct_hi = jnp.floor(ct * (1.0 / 256.0)) * 256.0
    c_ref[0] = (c - c_hi).astype(BF16)
    c_ref[1] = c_hi.astype(BF16)
    ct_ref[0] = (ct - ct_hi).astype(BF16)
    ct_ref[1] = ct_hi.astype(BF16)
    flag_ref[0, 0] = jnp.where(jnp.max(c) > 255.5, 1, 0).astype(jnp.int32)
    half = bs // 2
    for b in range(nbat):
        vals = jnp.swapaxes(v_ref[b].astype(F32), 0, 1)
        for h in range(2):
            part = vals[h * half : (h + 1) * half].reshape(half * kloc, npt)
            v2_ref[b, :, h * npt : (h + 1) * npt] = part.astype(BF16)
        for l in range(kloc):
            vt = jnp.transpose(v_ref[b, l].astype(F32))
            vt_ref[b, l] = jnp.concatenate([vt, vt], axis=1).astype(BF16)


def request_hot(req_ref, nblk):
    slabs, _, cap = req_ref.shape
    slots = slabs * cap
    req = req_ref[...].reshape(slabs, cap).astype(F32).astype(BF16)
    row = lax.broadcasted_iota(jnp.int32, (slots, slabs), 0) // cap
    col = lax.broadcasted_iota(jnp.int32, (slots, slabs), 1)
    spread = dot_nn(jnp.where(row == col, 1.0, 0.0).astype(BF16), req)
    nth = lax.broadcasted_iota(jnp.int32, (slots, cap), 0) % cap
    keep = lax.broadcasted_iota(jnp.int32, (slots, cap), 1) == nth
    ids = jnp.sum(jnp.where(keep, spread, 0.0), axis=1, keepdims=True).astype(jnp.int32)
    ids = jnp.broadcast_to(ids, (slots, nblk))
    same = lax.broadcasted_iota(jnp.int32, (slots, nblk), 1) == ids
    return jnp.where(same, 1.0, 0.0).astype(BF16)


def send_kernel(req_ref, own_ref, o_ref, hot_ref, buf, sem):
    slabs, rows, cap, _ = buf.shape
    hot = request_hot(req_ref, own_ref.shape[1])
    hot_ref[...] = hot
    group = rows // sem.shape[0]
    copies = []
    for jp in range(rows // 2):
        res = dot_nn(hot, own_ref[jp]).astype(BF16)
        buf[:, 2 * jp] = res[:, :LANES].reshape(slabs, cap, LANES)
        buf[:, 2 * jp + 1] = res[:, LANES:].reshape(slabs, cap, LANES)
        if (2 * jp + 2) % group == 0:
            n = len(copies)
            part = pl.ds(n * group, group)
            copies.append(pltpu.make_async_copy(buf.at[:, part], o_ref.at[:, part], sem.at[n]))
            copies[n].start()
    for copy in copies:
        copy.wait()


def slot_rows(ref, jp):
    slabs, _, cap, _ = ref.shape
    r0 = ref[:, 2 * jp].reshape(slabs * cap, LANES)
    r1 = ref[:, 2 * jp + 1].reshape(slabs * cap, LANES)
    return jnp.concatenate([r0, r1], axis=1)


def diagonal_values(v_ref, b):
    _, kloc, bs, npt = v_ref.shape
    zero = jnp.zeros((bs, npt), BF16)
    rows = []
    for l in range(kloc):
        v = v_ref[b, l]
        rows.append(jnp.concatenate([v, zero], axis=1))
        rows.append(jnp.concatenate([zero, v], axis=1))
    return jnp.concatenate(rows, axis=0)


def density_kernel(
    flag_ref, r_ref, c_hbm, v_hbm, v2_hbm, d_ref, c_ref, v_ref, v2_ref, hi_s, lo_s, sem
):
    nbat, kloc, _, npt = v_ref.shape
    rows = r_ref.shape[1]
    keys = c_ref.shape[1]
    get_c = [pltpu.make_async_copy(c_hbm.at[n], c_ref.at[n], sem.at[n]) for n in range(2)]
    get_v = pltpu.make_async_copy(v_hbm, v_ref, sem.at[2])
    get_v2 = pltpu.make_async_copy(v2_hbm, v2_ref, sem.at[3])
    get_c[0].start()
    get_v.start()
    get_v2.start()
    get_c[1].start()

    def build(jp, parts):
        rhs = slot_rows(r_ref, jp)
        res = dot_nn(c_ref[0], rhs)
        if parts == 2:
            res += dot_nn(c_ref[1], rhs)
        res = res.reshape(keys // SUB, SUB, 2 * LANES)
        hi, lo = split_pair(jnp.concatenate([res[:, :, :LANES], res[:, :, LANES:]], axis=1))
        at = pl.ds(pl.multiple_of(jp * 2 * SUB, 2 * SUB), 2 * SUB)
        hi_s[:, at, :] = hi
        lo_s[:, at, :] = lo

    get_c[0].wait()

    def loop(parts, group):
        def step(i, carry):
            for n in range(group):
                build(group * i + n, parts)
            return carry

        lax.fori_loop(0, rows // (2 * group), step, 0)

    @pl.when(flag_ref[0, 0] == 0)
    def _():
        loop(1, 8)

    get_c[1].wait()

    @pl.when(flag_ref[0, 0] != 0)
    def _():
        loop(2, 1)

    get_v.wait()
    get_v2.wait()

    def one_batch(b, carry):
        lhs = jnp.concatenate(
            [
                jnp.concatenate([hi_s[b * kloc + l] for l in range(kloc)], axis=1),
                jnp.concatenate([lo_s[b * kloc + l] for l in range(kloc)], axis=1),
            ],
            axis=0,
        )
        image = dot_nn(lhs, diagonal_values(v_ref, b))
        image = image[: rows * SUB] + image[rows * SUB :]
        d = jnp.sum(image * v2_ref[b].astype(F32), axis=0, keepdims=True)
        d_ref[pl.ds(b, 1), :] = d[:, :npt] + d[:, npt:]
        return carry

    lax.fori_loop(0, nbat, one_batch, 0, unroll=4)


def potential_kernel(
    flag_ref,
    mine_ref,
    other_ref,
    ct_ref,
    vt_ref,
    v2_ref,
    o_ref,
    d_ref,
    g_s,
    pot_s,
):
    nbat, kloc, npt, _ = vt_ref.shape
    low = lax.broadcasted_iota(jnp.int32, (npt, LANES), 1) < LANES // 2
    slabs, rows, cap, _ = o_ref.shape

    d = mine_ref[...] + other_ref[...]
    d_ref[...] = d
    pot = d / jnp.sqrt(1.0 + d * d)
    pot_s[...] = jnp.concatenate([pot, pot], axis=1)

    def one_batch(b):
        weighted = (v2_ref[b].astype(F32) * pot_s[pl.ds(b, 1), :]).astype(BF16)
        for lp in range(kloc // 2):
            pair = [vt_ref[b, 2 * lp], vt_ref[b, 2 * lp + 1]]
            zero = jnp.zeros_like(pair[0])
            top = jnp.concatenate([jnp.where(low, x, zero) for x in pair], axis=1)
            bottom = jnp.concatenate([jnp.where(low, zero, x) for x in pair], axis=1)
            rhs = jnp.concatenate([top, bottom], axis=0)
            g = dot_nn(weighted, rhs).reshape(rows, SUB, 2 * LANES)
            g = jnp.concatenate([g[:, :, :LANES], g[:, :, LANES:]], axis=1)
            row = pl.multiple_of((b * kloc + 2 * lp) * SUB, 2 * SUB)
            g_s[:, pl.ds(row, 2 * SUB), :] = g.astype(BF16)

    def some_batches(i, carry):
        for n in range(BATCH_GROUP):
            one_batch(i * BATCH_GROUP + n)
        return carry

    lax.fori_loop(0, nbat // BATCH_GROUP, some_batches, 0)

    def sums(jp, parts):
        rhs = jnp.concatenate([g_s[2 * jp], g_s[2 * jp + 1]], axis=1)
        out = dot_nn(ct_ref[0], rhs)
        if parts == 2:
            out += dot_nn(ct_ref[1], rhs)
        out = out.astype(BF16)
        o_ref[:, 2 * jp] = out[:, :LANES].reshape(slabs, cap, LANES)
        o_ref[:, 2 * jp + 1] = out[:, LANES:].reshape(slabs, cap, LANES)

    def loop(parts, group):
        def step(i, carry):
            for n in range(group):
                sums(group * i + n, parts)
            return carry

        lax.fori_loop(0, rows // (2 * group), step, 0)

    @pl.when(flag_ref[0, 0] == 0)
    def _():
        loop(1, 8)

    @pl.when(flag_ref[0, 0] != 0)
    def _():
        loop(2, 1)


def owner_kernel(hot_ref, ret_ref, o_ref):
    bs = o_ref.shape[2]
    half = o_ref.shape[1] // 2
    hot = hot_ref[...]
    for j in range(0, half, SUB):
        parts = []
        for jp in range(j // 2, (j + SUB) // 2):
            res = dot_nn(hot, slot_rows(ret_ref, jp))
            parts += [res[:, :LANES], res[:, LANES:]]
        sums = jnp.swapaxes(jnp.stack(parts, axis=0), 0, 1)
        o_ref[:, j : j + SUB] = sums[:, :, :bs]
        o_ref[:, half + j : half + j + SUB] = sums[:, :, bs:]


SMEM = pl.BlockSpec(memory_space=pltpu.SMEM)
VMEM = pl.BlockSpec(memory_space=pltpu.VMEM)
HBM = pl.BlockSpec(memory_space=pltpu.HBM)


def kernel_call(kernel, name, mib, **kwargs):
    params = pltpu.CompilerParams(vmem_limit_bytes=mib << 20)
    return pl.pallas_call(kernel, compiler_params=params, name=name, **kwargs)


def in_hbm(x):
    return pltpu.with_memory_space_constraint(x, pltpu.HBM)


def exchange(x):
    return lax.all_to_all(x, "slab", split_axis=0, concat_axis=0, tiled=True)


def body(p_blocks, basis_vals, need_list, tasks, task_counts):
    own = p_blocks[0]
    blk_dev, bs, _ = own.shape
    nbat, kloc, _, npt = basis_vals.shape
    slabs, cap = need_list.shape[2:]
    slots = slabs * cap
    half = bs // 2
    keys = nbat * kloc * kloc
    wide = jax.ShapeDtypeStruct((slabs, half, cap, LANES), BF16)

    wanted = kernel_call(
        turn_kernel,
        "turn",
        4,
        out_shape=jax.ShapeDtypeStruct((slabs, 1, cap), jnp.int32),
        in_specs=[VMEM],
        out_specs=VMEM,
    )(need_list[0, 0].T)
    requested = exchange(wanted)

    own_rows = kernel_call(
        own_kernel,
        "own",
        8,
        out_shape=jax.ShapeDtypeStruct((half // 2, blk_dev, 2 * LANES), BF16),
        in_specs=[VMEM],
        out_specs=VMEM,
    )(own)

    sent, hot = kernel_call(
        send_kernel,
        "send",
        8,
        out_shape=(pltpu.HBM(wide.shape, BF16), jax.ShapeDtypeStruct((slots, blk_dev), BF16)),
        in_specs=[VMEM, VMEM],
        out_specs=(HBM, VMEM),
        scratch_shapes=[pltpu.VMEM(wide.shape, BF16), pltpu.SemaphoreType.DMA((4,))],
    )(requested, own_rows)
    received = exchange(sent)

    counts, counts_t, v2, vt, hot_t, flag = kernel_call(
        prep_kernel,
        "prep",
        24,
        out_shape=(
            jax.ShapeDtypeStruct((2, keys, slots), BF16),
            jax.ShapeDtypeStruct((2, slots, keys), BF16),
            jax.ShapeDtypeStruct((nbat, half * kloc, 2 * npt), BF16),
            jax.ShapeDtypeStruct((nbat, kloc, npt, LANES), BF16),
            jax.ShapeDtypeStruct((blk_dev, slots), BF16),
            jax.ShapeDtypeStruct((1, 1), jnp.int32),
        ),
        in_specs=[SMEM, VMEM, VMEM, VMEM],
        out_specs=(VMEM, VMEM, VMEM, VMEM, VMEM, SMEM),
    )(task_counts, tasks[0, 0], basis_vals, hot)

    partial = kernel_call(
        density_kernel,
        "density",
        16,
        out_shape=jax.ShapeDtypeStruct((nbat, npt), F32),
        in_specs=[SMEM, VMEM, HBM, HBM, HBM],
        out_specs=VMEM,
        scratch_shapes=[
            pltpu.VMEM(counts.shape, BF16),
            pltpu.VMEM(basis_vals.shape, BF16),
            pltpu.VMEM(v2.shape, BF16),
        ]
        + [pltpu.VMEM((nbat * kloc, half * SUB, LANES), BF16)] * 2
        + [pltpu.SemaphoreType.DMA((4,))],
    )(flag, received, in_hbm(counts), in_hbm(basis_vals), in_hbm(v2))
    swap = [(0, 1), (1, 0)]
    other = lax.ppermute(partial, "blk", swap)

    slot_sums, density = kernel_call(
        potential_kernel,
        "potential",
        24,
        out_shape=(wide, jax.ShapeDtypeStruct((nbat, npt), F32)),
        in_specs=[SMEM] + [VMEM] * 5,
        out_specs=(VMEM, VMEM),
        scratch_shapes=[
            pltpu.VMEM((half, keys, LANES), BF16),
            pltpu.VMEM((nbat, 2 * npt), F32),
        ],
    )(flag, partial, other, counts_t, vt, v2)
    returned = exchange(slot_sums)

    owner_sums = kernel_call(
        owner_kernel,
        "owner",
        8,
        out_shape=jax.ShapeDtypeStruct((blk_dev, bs, bs), F32),
        in_specs=[VMEM, VMEM],
        out_specs=VMEM,
    )(hot_t, returned)
    return (density, owner_sums[None])


def solution(mesh):
    in_specs = (
        P("blk", "slab", None, None),
        P("slab", None, None, None),
        P("blk", "slab", None, None),
        P("blk", "slab", None, None),
        P("blk", "slab"),
    )
    out_specs = (P("slab", None), P("blk", "slab", None, None))
    return jax.shard_map(body, mesh=mesh, in_specs=in_specs, out_specs=out_specs, check_vma=False)
```

```python
import jax
import jax.numpy as jnp
from jax import lax
from jax.experimental import pallas as pl
from jax.experimental.pallas import tpu as pltpu
from jax.sharding import PartitionSpec as P


F32 = jnp.float32
BF16 = jnp.bfloat16
LANES = 128
SUB = 8
TASK_STEP = 512
BATCH_GROUP = 4


def dot_nn(a, b):
    return lax.dot_general(a, b, (((1,), (0,)), ((), ())), preferred_element_type=F32)


def dot_nt(a, b):
    return lax.dot_general(a, b, (((1,), (1,)), ((), ())), preferred_element_type=F32)


def split_pair(x):
    hi = x.astype(BF16)
    return hi, (x - hi.astype(F32)).astype(BF16)


def turn_kernel(x_ref, o_ref):
    x = jnp.transpose(x_ref[...])
    o_ref[...] = x.reshape(o_ref.shape)


def own_kernel(own_ref, o_ref):
    half = own_ref.shape[1] // 2
    own = own_ref[...].astype(F32)
    own = jnp.concatenate([own[:, :half], own[:, half:]], axis=2)
    own = jnp.swapaxes(own, 0, 1).astype(BF16)
    for j in range(half):
        o_ref[j // 2, :, (j % 2) * LANES : (j % 2 + 1) * LANES] = own[j]


def prep_kernel(
    count_ref, tasks_ref, v_ref, c_ref, c_hi_ref, ct_ref, ct_hi_ref, v2_ref, vt_ref, flag_ref
):
    nbat, kloc, bs, npt = v_ref.shape
    keys = nbat * kloc * kloc
    slots = c_ref.shape[1]
    tcap = tasks_ref.shape[1]
    step = TASK_STEP if tcap % TASK_STEP == 0 else tcap
    live = count_ref[0, 0]
    c = jnp.zeros((keys, slots), F32)
    ct = jnp.zeros((slots, keys), F32)
    for t in range(0, tcap, step):
        fields = tasks_ref[:, t : t + step]
        key = (fields[0:1] * kloc + fields[2:3]) * kloc + fields[1:2]
        lane = lax.broadcasted_iota(jnp.int32, (1, step), 1) + t
        key = jnp.where(lane < live, key, -1)
        key_hot = jnp.where(
            lax.broadcasted_iota(jnp.int32, (keys, step), 0) == key, 1.0, 0.0
        ).astype(BF16)
        slot_hot = jnp.where(
            lax.broadcasted_iota(jnp.int32, (slots, step), 0) == fields[3:4], 1.0, 0.0
        ).astype(BF16)
        c += dot_nt(key_hot, slot_hot)
        ct += dot_nt(slot_hot, key_hot)
    c_hi = jnp.floor(c * (1.0 / 256.0)) * 256.0
    ct_hi = jnp.floor(ct * (1.0 / 256.0)) * 256.0
    c_ref[...] = (c - c_hi).astype(BF16)
    c_hi_ref[...] = c_hi.astype(BF16)
    ct_ref[...] = (ct - ct_hi).astype(BF16)
    ct_hi_ref[...] = ct_hi.astype(BF16)
    flag_ref[0, 0] = jnp.where(jnp.max(c) > 255.5, 1, 0).astype(jnp.int32)
    half = bs // 2
    for b in range(nbat):
        vals = jnp.swapaxes(v_ref[b].astype(F32), 0, 1)
        for h in range(2):
            part = vals[h * half : (h + 1) * half].reshape(half * kloc, npt)
            v2_ref[b, :, h * npt : (h + 1) * npt] = part.astype(BF16)
        for l in range(kloc):
            vt = jnp.transpose(v_ref[b, l].astype(F32))
            vt_ref[b, l] = jnp.concatenate([vt, vt], axis=1).astype(BF16)


def request_hot(req_ref, nblk):
    slabs, _, cap = req_ref.shape
    slots = slabs * cap
    req = req_ref[...].reshape(slabs, cap).astype(F32).astype(BF16)
    row = lax.broadcasted_iota(jnp.int32, (slots, slabs), 0) // cap
    col = lax.broadcasted_iota(jnp.int32, (slots, slabs), 1)
    spread = dot_nn(jnp.where(row == col, 1.0, 0.0).astype(BF16), req)
    nth = lax.broadcasted_iota(jnp.int32, (slots, cap), 0) % cap
    keep = lax.broadcasted_iota(jnp.int32, (slots, cap), 1) == nth
    ids = jnp.sum(jnp.where(keep, spread, 0.0), axis=1, keepdims=True).astype(jnp.int32)
    ids = jnp.broadcast_to(ids, (slots, nblk))
    same = lax.broadcasted_iota(jnp.int32, (slots, nblk), 1) == ids
    return jnp.where(same, 1.0, 0.0).astype(BF16)


def send_kernel(req_ref, own_ref, o_ref, hot_ref, buf, sem):
    slabs, rows, cap, _ = buf.shape
    hot = request_hot(req_ref, own_ref.shape[1])
    hot_ref[...] = hot
    group = rows // sem.shape[0]
    copies = []
    for jp in range(rows // 2):
        res = dot_nn(hot, own_ref[jp]).astype(BF16)
        buf[:, 2 * jp] = res[:, :LANES].reshape(slabs, cap, LANES)
        buf[:, 2 * jp + 1] = res[:, LANES:].reshape(slabs, cap, LANES)
        if (2 * jp + 2) % group == 0:
            n = len(copies)
            part = pl.ds(n * group, group)
            copies.append(pltpu.make_async_copy(buf.at[:, part], o_ref.at[:, part], sem.at[n]))
            copies[n].start()
    for copy in copies:
        copy.wait()


def slot_rows(ref, jp):
    slabs, _, cap, _ = ref.shape
    r0 = ref[:, 2 * jp].reshape(slabs * cap, LANES)
    r1 = ref[:, 2 * jp + 1].reshape(slabs * cap, LANES)
    return jnp.concatenate([r0, r1], axis=1)


def diagonal_values(v_ref, b):
    _, kloc, bs, npt = v_ref.shape
    zero = jnp.zeros((bs, npt), BF16)
    rows = []
    for l in range(kloc):
        v = v_ref[b, l]
        rows.append(jnp.concatenate([v, zero], axis=1))
        rows.append(jnp.concatenate([zero, v], axis=1))
    return jnp.concatenate(rows, axis=0)


def density_kernel(
    flag_ref, r_ref, c_ref, c_hbm, v_hbm, v2_hbm, d_ref, c_hi_ref, v_ref, v2_ref, hi_s, lo_s, sem
):
    nbat, kloc, _, npt = v_ref.shape
    rows = r_ref.shape[1]
    keys = c_ref.shape[0]
    get_c = pltpu.make_async_copy(c_hbm, c_hi_ref, sem.at[0])
    get_v = pltpu.make_async_copy(v_hbm, v_ref, sem.at[1])
    get_v2 = pltpu.make_async_copy(v2_hbm, v2_ref, sem.at[2])
    get_v.start()
    get_v2.start()

    def build(jp, parts):
        rhs = slot_rows(r_ref, jp)
        res = dot_nn(c_ref[...], rhs)
        if parts == 2:
            res += dot_nn(c_hi_ref[...], rhs)
        res = res.reshape(keys // SUB, SUB, 2 * LANES)
        hi, lo = split_pair(jnp.concatenate([res[:, :, :LANES], res[:, :, LANES:]], axis=1))
        at = pl.ds(pl.multiple_of(jp * 2 * SUB, 2 * SUB), 2 * SUB)
        hi_s[:, at, :] = hi
        lo_s[:, at, :] = lo

    def loop(parts, group):
        def step(i, carry):
            for n in range(group):
                build(group * i + n, parts)
            return carry

        lax.fori_loop(0, rows // (2 * group), step, 0)

    @pl.when(flag_ref[0, 0] == 0)
    def _():
        loop(1, 8)

    @pl.when(flag_ref[0, 0] != 0)
    def _():
        get_c.start()
        get_c.wait()
        loop(2, 1)

    get_v.wait()
    get_v2.wait()

    def one_batch(b, carry):
        lhs = jnp.concatenate(
            [
                jnp.concatenate([hi_s[b * kloc + l] for l in range(kloc)], axis=1),
                jnp.concatenate([lo_s[b * kloc + l] for l in range(kloc)], axis=1),
            ],
            axis=0,
        )
        image = dot_nn(lhs, diagonal_values(v_ref, b))
        image = image[: rows * SUB] + image[rows * SUB :]
        d = jnp.sum(image * v2_ref[b].astype(F32), axis=0, keepdims=True)
        d_ref[pl.ds(b, 1), :] = d[:, :npt] + d[:, npt:]
        return carry

    lax.fori_loop(0, nbat, one_batch, 0, unroll=4)


def potential_kernel(
    flag_ref,
    mine_ref,
    other_ref,
    ct_ref,
    ct_hbm,
    vt_ref,
    v2_ref,
    o_ref,
    d_ref,
    g_s,
    pot_s,
    ct_hi_ref,
    buf,
    sem,
    out_sem,
):
    nbat, kloc, npt, _ = vt_ref.shape
    low = lax.broadcasted_iota(jnp.int32, (npt, LANES), 1) < LANES // 2
    slabs, rows, cap, _ = o_ref.shape

    d = mine_ref[...] + other_ref[...]
    d_ref[...] = d
    pot = d / jnp.sqrt(1.0 + d * d)
    pot_s[...] = jnp.concatenate([pot, pot], axis=1)

    def one_batch(b):
        weighted = (v2_ref[b].astype(F32) * pot_s[pl.ds(b, 1), :]).astype(BF16)
        for lp in range(kloc // 2):
            pair = [vt_ref[b, 2 * lp], vt_ref[b, 2 * lp + 1]]
            zero = jnp.zeros_like(pair[0])
            top = jnp.concatenate([jnp.where(low, x, zero) for x in pair], axis=1)
            bottom = jnp.concatenate([jnp.where(low, zero, x) for x in pair], axis=1)
            rhs = jnp.concatenate([top, bottom], axis=0)
            g = dot_nn(weighted, rhs).reshape(rows, SUB, 2 * LANES)
            g = jnp.concatenate([g[:, :, :LANES], g[:, :, LANES:]], axis=1)
            row = pl.multiple_of((b * kloc + 2 * lp) * SUB, 2 * SUB)
            g_s[:, pl.ds(row, 2 * SUB), :] = g.astype(BF16)

    def some_batches(i, carry):
        for n in range(BATCH_GROUP):
            one_batch(i * BATCH_GROUP + n)
        return carry

    lax.fori_loop(0, nbat // BATCH_GROUP, some_batches, 0)

    def sums(jp, parts):
        rhs = jnp.concatenate([g_s[2 * jp], g_s[2 * jp + 1]], axis=1)
        out = dot_nn(ct_ref[...], rhs)
        if parts == 2:
            out += dot_nn(ct_hi_ref[...], rhs)
        out = out.astype(BF16)
        buf[:, 2 * jp] = out[:, :LANES].reshape(slabs, cap, LANES)
        buf[:, 2 * jp + 1] = out[:, LANES:].reshape(slabs, cap, LANES)

    width = rows // out_sem.shape[0]

    def put(n):
        part = pl.ds(n * width, width)
        return pltpu.make_async_copy(buf.at[:, part], o_ref.at[:, part], out_sem.at[n])

    def loop(parts, group):
        def step(i, carry):
            for n in range(group):
                sums(group * i + n, parts)
                if (n + 1) % (width // 2) == 0:
                    put((group * i + n) // (width // 2)).start()
            return carry

        lax.fori_loop(0, rows // (2 * group), step, 0)

    @pl.when(flag_ref[0, 0] == 0)
    def _():
        loop(1, 8)

    @pl.when(flag_ref[0, 0] != 0)
    def _():
        get_ct = pltpu.make_async_copy(ct_hbm, ct_hi_ref, sem.at[0])
        get_ct.start()
        get_ct.wait()
        loop(2, width // 2)

    for n in range(out_sem.shape[0]):
        put(n).wait()


def flip_kernel(hot_ref, o_ref):
    o_ref[...] = jnp.transpose(hot_ref[...].astype(F32)).astype(BF16)


def owner_kernel(hot_ref, ret_ref, o_ref):
    bs = o_ref.shape[2]
    half = o_ref.shape[1] // 2
    hot = hot_ref[...]
    for j in range(0, half, SUB):
        parts = []
        for jp in range(j // 2, (j + SUB) // 2):
            res = dot_nn(hot, slot_rows(ret_ref, jp))
            parts += [res[:, :LANES], res[:, LANES:]]
        sums = jnp.swapaxes(jnp.stack(parts, axis=0), 0, 1)
        o_ref[:, j : j + SUB] = sums[:, :, :bs]
        o_ref[:, half + j : half + j + SUB] = sums[:, :, bs:]


SMEM = pl.BlockSpec(memory_space=pltpu.SMEM)
VMEM = pl.BlockSpec(memory_space=pltpu.VMEM)
HBM = pl.BlockSpec(memory_space=pltpu.HBM)


def kernel_call(kernel, mib, **kwargs):
    params = pltpu.CompilerParams(vmem_limit_bytes=mib << 20)
    return pl.pallas_call(kernel, compiler_params=params, **kwargs)


def in_hbm(x):
    return pltpu.with_memory_space_constraint(x, pltpu.HBM)


def exchange(x):
    return lax.all_to_all(x, "slab", split_axis=0, concat_axis=0, tiled=True)


def body(p_blocks, basis_vals, need_list, tasks, task_counts):
    own = p_blocks[0]
    blk_dev, bs, _ = own.shape
    nbat, kloc, _, npt = basis_vals.shape
    slabs, cap = need_list.shape[2:]
    slots = slabs * cap
    half = bs // 2
    keys = nbat * kloc * kloc
    wide = jax.ShapeDtypeStruct((slabs, half, cap, LANES), BF16)

    wanted = kernel_call(
        turn_kernel,
        4,
        out_shape=jax.ShapeDtypeStruct((slabs, 1, cap), jnp.int32),
        in_specs=[VMEM],
        out_specs=VMEM,
    )(need_list[0, 0].T)
    requested = exchange(wanted)

    own_rows = kernel_call(
        own_kernel,
        8,
        out_shape=jax.ShapeDtypeStruct((half // 2, blk_dev, 2 * LANES), BF16),
        in_specs=[VMEM],
        out_specs=VMEM,
    )(own)

    sent, hot = kernel_call(
        send_kernel,
        8,
        out_shape=(pltpu.HBM(wide.shape, BF16), jax.ShapeDtypeStruct((slots, blk_dev), BF16)),
        in_specs=[VMEM, VMEM],
        out_specs=(HBM, VMEM),
        scratch_shapes=[pltpu.VMEM(wide.shape, BF16), pltpu.SemaphoreType.DMA((4,))],
    )(requested, own_rows)
    received = exchange(sent)

    counts, counts_hi, counts_t, counts_t_hi, v2, vt, flag = kernel_call(
        prep_kernel,
        24,
        out_shape=(
            jax.ShapeDtypeStruct((keys, slots), BF16),
            jax.ShapeDtypeStruct((keys, slots), BF16),
            jax.ShapeDtypeStruct((slots, keys), BF16),
            jax.ShapeDtypeStruct((slots, keys), BF16),
            jax.ShapeDtypeStruct((nbat, half * kloc, 2 * npt), BF16),
            jax.ShapeDtypeStruct((nbat, kloc, npt, LANES), BF16),
            jax.ShapeDtypeStruct((1, 1), jnp.int32),
        ),
        in_specs=[SMEM, VMEM, VMEM],
        out_specs=(VMEM,) * 6 + (SMEM,),
    )(task_counts, tasks[0, 0], basis_vals)

    partial = kernel_call(
        density_kernel,
        16,
        out_shape=jax.ShapeDtypeStruct((nbat, npt), F32),
        in_specs=[SMEM, VMEM, VMEM, HBM, HBM, HBM],
        out_specs=VMEM,
        scratch_shapes=[
            pltpu.VMEM(counts.shape, BF16),
            pltpu.VMEM(basis_vals.shape, BF16),
            pltpu.VMEM(v2.shape, BF16),
        ]
        + [pltpu.VMEM((nbat * kloc, half * SUB, LANES), BF16)] * 2
        + [pltpu.SemaphoreType.DMA((3,))],
    )(flag, received, counts, in_hbm(counts_hi), in_hbm(basis_vals), in_hbm(v2))
    swap = [(0, 1), (1, 0)]
    other = lax.ppermute(partial, "blk", swap)

    slot_sums, density = kernel_call(
        potential_kernel,
        24,
        out_shape=(pltpu.HBM(wide.shape, BF16), jax.ShapeDtypeStruct((nbat, npt), F32)),
        in_specs=[SMEM, VMEM, VMEM, VMEM, HBM, VMEM, VMEM],
        out_specs=(HBM, VMEM),
        scratch_shapes=[
            pltpu.VMEM((half, keys, LANES), BF16),
            pltpu.VMEM((nbat, 2 * npt), F32),
            pltpu.VMEM(counts_t.shape, BF16),
            pltpu.VMEM(wide.shape, BF16),
            pltpu.SemaphoreType.DMA((1,)),
            pltpu.SemaphoreType.DMA((4,)),
        ],
    )(flag, partial, other, counts_t, in_hbm(counts_t_hi), vt, v2)
    returned = exchange(slot_sums)
    hot_t = kernel_call(
        flip_kernel,
        4,
        out_shape=jax.ShapeDtypeStruct((blk_dev, slots), BF16),
        in_specs=[VMEM],
        out_specs=VMEM,
    )(hot)

    owner_sums = kernel_call(
        owner_kernel,
        8,
        out_shape=jax.ShapeDtypeStruct((blk_dev, bs, bs), F32),
        in_specs=[VMEM, VMEM],
        out_specs=VMEM,
    )(hot_t, returned)
    return (density, owner_sums[None])


def solution(mesh):
    in_specs = (
        P("blk", "slab", None, None),
        P("slab", None, None, None),
        P("blk", "slab", None, None),
        P("blk", "slab", None, None),
        P("blk", "slab"),
    )
    out_specs = (P("slab", None), P("blk", "slab", None, None))
    return jax.shard_map(body, mesh=mesh, in_specs=in_specs, out_specs=out_specs, check_vma=False)
```

```python
import jax
import jax.numpy as jnp
from jax import lax
from jax.experimental import pallas as pl
from jax.experimental.pallas import tpu as pltpu
from jax.sharding import PartitionSpec as P

F32 = jnp.float32
BF16 = jnp.bfloat16
LANES = 128
SUB = 8
TASK_STEP = 512
GROUP = 4
BATCH_GROUP = 4


def dot_nn(a, b):
    return lax.dot_general(a, b, (((1,), (0,)), ((), ())), preferred_element_type=F32)


def dot_nt(a, b):
    return lax.dot_general(a, b, (((1,), (1,)), ((), ())), preferred_element_type=F32)


def split_pair(x):
    hi = x.astype(BF16)
    return hi, (x - hi.astype(F32)).astype(BF16)


def turn_kernel(x_ref, o_ref):
    x = jnp.transpose(x_ref[...])
    o_ref[...] = x.reshape(o_ref.shape)


def own_kernel(own_ref, o_ref):
    half = own_ref.shape[1] // 2
    own = own_ref[...].astype(F32)
    own = jnp.concatenate([own[:, :half], own[:, half:]], axis=2)
    own = jnp.swapaxes(own, 0, 1).astype(BF16)
    for j in range(half):
        o_ref[j // 2, :, (j % 2) * LANES : (j % 2 + 1) * LANES] = own[j]


def prep_kernel(
    count_ref, tasks_ref, v_ref, hot_ref, c_ref, c_hi_ref, ct_ref, ct_hi_ref, v2_ref, vt_ref, hot_t_ref, flag_ref
):
    hot_t_ref[...] = jnp.transpose(hot_ref[...].astype(F32)).astype(BF16)
    nbat, kloc, bs, npt = v_ref.shape
    keys = nbat * kloc * kloc
    slots = c_ref.shape[1]
    tcap = tasks_ref.shape[1]
    step = TASK_STEP if tcap % TASK_STEP == 0 else tcap
    live = count_ref[0, 0]
    c = jnp.zeros((keys, slots), F32)
    ct = jnp.zeros((slots, keys), F32)
    for t in range(0, tcap, step):
        fields = tasks_ref[:, t : t + step]
        key = (fields[0:1] * kloc + fields[2:3]) * kloc + fields[1:2]
        lane = lax.broadcasted_iota(jnp.int32, (1, step), 1) + t
        key = jnp.where(lane < live, key, -1)
        key_hot = jnp.where(
            lax.broadcasted_iota(jnp.int32, (keys, step), 0) == key, 1.0, 0.0
        ).astype(BF16)
        slot_hot = jnp.where(
            lax.broadcasted_iota(jnp.int32, (slots, step), 0) == fields[3:4], 1.0, 0.0
        ).astype(BF16)
        c += dot_nt(key_hot, slot_hot)
        ct += dot_nt(slot_hot, key_hot)
    c_hi = jnp.floor(c * (1.0 / 256.0)) * 256.0
    ct_hi = jnp.floor(ct * (1.0 / 256.0)) * 256.0
    c_ref[...] = (c - c_hi).astype(BF16)
    c_hi_ref[...] = c_hi.astype(BF16)
    ct_ref[...] = (ct - ct_hi).astype(BF16)
    ct_hi_ref[...] = ct_hi.astype(BF16)
    flag_ref[0, 0] = jnp.where(jnp.max(c) > 255.5, 1, 0).astype(jnp.int32)
    half = bs // 2
    for b in range(nbat):
        vals = jnp.swapaxes(v_ref[b].astype(F32), 0, 1)
        for h in range(2):
            part = vals[h * half : (h + 1) * half].reshape(half * kloc, npt)
            v2_ref[b, :, h * npt : (h + 1) * npt] = part.astype(BF16)
        for l in range(kloc):
            vt = jnp.transpose(v_ref[b, l].astype(F32))
            vt_ref[b, l] = jnp.concatenate([vt, vt], axis=1).astype(BF16)


def request_hot(req_ref, nblk):
    slabs, _, cap = req_ref.shape
    slots = slabs * cap
    req = req_ref[...].reshape(slabs, cap).astype(F32).astype(BF16)
    row = lax.broadcasted_iota(jnp.int32, (slots, slabs), 0) // cap
    col = lax.broadcasted_iota(jnp.int32, (slots, slabs), 1)
    spread = dot_nn(jnp.where(row == col, 1.0, 0.0).astype(BF16), req)
    nth = lax.broadcasted_iota(jnp.int32, (slots, cap), 0) % cap
    keep = lax.broadcasted_iota(jnp.int32, (slots, cap), 1) == nth
    ids = jnp.sum(jnp.where(keep, spread, 0.0), axis=1, keepdims=True).astype(jnp.int32)
    ids = jnp.broadcast_to(ids, (slots, nblk))
    same = lax.broadcasted_iota(jnp.int32, (slots, nblk), 1) == ids
    return jnp.where(same, 1.0, 0.0).astype(BF16)


def send_kernel(req_ref, own_ref, o_ref, hot_ref, buf, sem):
    slabs, rows, cap, _ = buf.shape
    hot = request_hot(req_ref, own_ref.shape[1])
    hot_ref[...] = hot
    group = rows // sem.shape[0]
    copies = []
    for jp in range(rows // 2):
        res = dot_nn(hot, own_ref[jp]).astype(BF16)
        buf[:, 2 * jp] = res[:, :LANES].reshape(slabs, cap, LANES)
        buf[:, 2 * jp + 1] = res[:, LANES:].reshape(slabs, cap, LANES)
        if (2 * jp + 2) % group == 0:
            n = len(copies)
            part = pl.ds(n * group, group)
            copies.append(pltpu.make_async_copy(buf.at[:, part], o_ref.at[:, part], sem.at[n]))
            copies[n].start()
    for copy in copies:
        copy.wait()


def slot_rows(ref, jp):
    slabs, _, cap, _ = ref.shape
    r0 = ref[:, 2 * jp].reshape(slabs * cap, LANES)
    r1 = ref[:, 2 * jp + 1].reshape(slabs * cap, LANES)
    return jnp.concatenate([r0, r1], axis=1)


def diagonal_values(v_ref, b):
    _, kloc, bs, npt = v_ref.shape
    zero = jnp.zeros((bs, npt), BF16)
    rows = []
    for l in range(kloc):
        v = v_ref[b, l]
        rows.append(jnp.concatenate([v, zero], axis=1))
        rows.append(jnp.concatenate([zero, v], axis=1))
    return jnp.concatenate(rows, axis=0)


def density_kernel(
    flag_ref, r_ref, c_ref, c_hbm, v_hbm, v2_hbm, d_ref, c_hi_ref, v_ref, v2_ref, hi_s, lo_s, sem
):
    nbat, kloc, _, npt = v_ref.shape
    rows = r_ref.shape[1]
    keys = c_ref.shape[0]
    get_c = pltpu.make_async_copy(c_hbm, c_hi_ref, sem.at[0])
    get_v = pltpu.make_async_copy(v_hbm, v_ref, sem.at[1])
    get_v2 = pltpu.make_async_copy(v2_hbm, v2_ref, sem.at[2])
    get_v.start()
    get_v2.start()

    def build(jp, parts):
        rhs = slot_rows(r_ref, jp)
        res = dot_nn(c_ref[...], rhs)
        if parts == 2:
            res += dot_nn(c_hi_ref[...], rhs)
        res = res.reshape(keys // SUB, SUB, 2 * LANES)
        hi, lo = split_pair(jnp.concatenate([res[:, :, :LANES], res[:, :, LANES:]], axis=1))
        at = pl.ds(pl.multiple_of(jp * 2 * SUB, 2 * SUB), 2 * SUB)
        hi_s[:, at, :] = hi
        lo_s[:, at, :] = lo

    def loop(parts, group):
        def step(i, carry):
            for n in range(group):
                build(group * i + n, parts)
            return carry

        lax.fori_loop(0, rows // (2 * group), step, 0)

    @pl.when(flag_ref[0, 0] == 0)
    def _():
        loop(1, 8)

    @pl.when(flag_ref[0, 0] != 0)
    def _():
        get_c.start()
        get_c.wait()
        loop(2, 1)

    get_v.wait()
    get_v2.wait()

    def one_batch(b, carry):
        lhs = jnp.concatenate(
            [
                jnp.concatenate([hi_s[b * kloc + l] for l in range(kloc)], axis=1),
                jnp.concatenate([lo_s[b * kloc + l] for l in range(kloc)], axis=1),
            ],
            axis=0,
        )
        image = dot_nn(lhs, diagonal_values(v_ref, b))
        image = image[: rows * SUB] + image[rows * SUB :]
        d = jnp.sum(image * v2_ref[b].astype(F32), axis=0, keepdims=True)
        d_ref[pl.ds(b, 1), :] = d[:, :npt] + d[:, npt:]
        return carry

    lax.fori_loop(0, nbat, one_batch, 0, unroll=4)


def potential_kernel(
    flag_ref,
    mine_ref,
    other_ref,
    ct_ref,
    ct_hbm,
    vt_ref,
    v2_ref,
    o_ref,
    d_ref,
    g_s,
    pot_s,
    ct_hi_ref,
    sem,
):
    nbat, kloc, npt, _ = vt_ref.shape
    low = lax.broadcasted_iota(jnp.int32, (npt, LANES), 1) < LANES // 2
    slabs, rows, cap, _ = o_ref.shape

    d = mine_ref[...] + other_ref[...]
    d_ref[...] = d
    pot = d / jnp.sqrt(1.0 + d * d)
    pot_s[...] = jnp.concatenate([pot, pot], axis=1)

    def one_batch(b):
        weighted = (v2_ref[b].astype(F32) * pot_s[pl.ds(b, 1), :]).astype(BF16)
        for lp in range(kloc // 2):
            pair = [vt_ref[b, 2 * lp], vt_ref[b, 2 * lp + 1]]
            zero = jnp.zeros_like(pair[0])
            top = jnp.concatenate([jnp.where(low, x, zero) for x in pair], axis=1)
            bottom = jnp.concatenate([jnp.where(low, zero, x) for x in pair], axis=1)
            rhs = jnp.concatenate([top, bottom], axis=0)
            g = dot_nn(weighted, rhs).reshape(rows, SUB, 2 * LANES)
            g = jnp.concatenate([g[:, :, :LANES], g[:, :, LANES:]], axis=1)
            row = pl.multiple_of((b * kloc + 2 * lp) * SUB, 2 * SUB)
            g_s[:, pl.ds(row, 2 * SUB), :] = g.astype(BF16)

    def some_batches(i, carry):
        for n in range(BATCH_GROUP):
            one_batch(i * BATCH_GROUP + n)
        return carry

    lax.fori_loop(0, nbat // BATCH_GROUP, some_batches, 0)

    def sums(jp, parts):
        rhs = jnp.concatenate([g_s[2 * jp], g_s[2 * jp + 1]], axis=1)
        out = dot_nn(ct_ref[...], rhs)
        if parts == 2:
            out += dot_nn(ct_hi_ref[...], rhs)
        out = out.astype(BF16)
        o_ref[:, 2 * jp] = out[:, :LANES].reshape(slabs, cap, LANES)
        o_ref[:, 2 * jp + 1] = out[:, LANES:].reshape(slabs, cap, LANES)

    def loop(parts, group):
        def step(i, carry):
            for n in range(group):
                sums(group * i + n, parts)
            return carry

        lax.fori_loop(0, rows // (2 * group), step, 0)

    @pl.when(flag_ref[0, 0] == 0)
    def _():
        loop(1, 8)

    @pl.when(flag_ref[0, 0] != 0)
    def _():
        get_ct = pltpu.make_async_copy(ct_hbm, ct_hi_ref, sem.at[0])
        get_ct.start()
        get_ct.wait()
        loop(2, 1)


def owner_kernel(hot_ref, ret_ref, o_ref):
    bs = o_ref.shape[2]
    half = o_ref.shape[1] // 2
    hot = hot_ref[...]
    for j in range(0, half, SUB):
        parts = []
        for jp in range(j // 2, (j + SUB) // 2):
            res = dot_nn(hot, slot_rows(ret_ref, jp))
            parts += [res[:, :LANES], res[:, LANES:]]
        sums = jnp.swapaxes(jnp.stack(parts, axis=0), 0, 1)
        o_ref[:, j : j + SUB] = sums[:, :, :bs]
        o_ref[:, half + j : half + j + SUB] = sums[:, :, bs:]


SMEM = pl.BlockSpec(memory_space=pltpu.SMEM)
VMEM = pl.BlockSpec(memory_space=pltpu.VMEM)
HBM = pl.BlockSpec(memory_space=pltpu.HBM)


def kernel_call(kernel, name, mib, **kwargs):
    params = pltpu.CompilerParams(vmem_limit_bytes=mib << 20)
    return pl.pallas_call(kernel, compiler_params=params, name=name, **kwargs)


def in_hbm(x):
    return pltpu.with_memory_space_constraint(x, pltpu.HBM)


def exchange(x):
    return lax.all_to_all(x, "slab", split_axis=0, concat_axis=0, tiled=True)


def body(p_blocks, basis_vals, need_list, tasks, task_counts):
    own = p_blocks[0]
    blk_dev, bs, _ = own.shape
    nbat, kloc, _, npt = basis_vals.shape
    slabs, cap = need_list.shape[2:]
    slots = slabs * cap
    half = bs // 2
    keys = nbat * kloc * kloc
    wide = jax.ShapeDtypeStruct((slabs, half, cap, LANES), BF16)

    wanted = kernel_call(
        turn_kernel,
        "turn",
        4,
        out_shape=jax.ShapeDtypeStruct((slabs, 1, cap), jnp.int32),
        in_specs=[VMEM],
        out_specs=VMEM,
    )(need_list[0, 0].T)
    requested = exchange(wanted)

    own_rows = kernel_call(
        own_kernel,
        "own",
        8,
        out_shape=jax.ShapeDtypeStruct((half // 2, blk_dev, 2 * LANES), BF16),
        in_specs=[VMEM],
        out_specs=VMEM,
    )(own)

    sent, hot = kernel_call(
        send_kernel,
        "send",
        8,
        out_shape=(pltpu.HBM(wide.shape, BF16), jax.ShapeDtypeStruct((slots, blk_dev), BF16)),
        in_specs=[VMEM, VMEM],
        out_specs=(HBM, VMEM),
        scratch_shapes=[pltpu.VMEM(wide.shape, BF16), pltpu.SemaphoreType.DMA((4,))],
    )(requested, own_rows)
    received = exchange(sent)

    counts, counts_hi, counts_t, counts_t_hi, v2, vt, hot_t, flag = kernel_call(
        prep_kernel,
        "prep",
        24,
        out_shape=(
            jax.ShapeDtypeStruct((keys, slots), BF16),
            jax.ShapeDtypeStruct((keys, slots), BF16),
            jax.ShapeDtypeStruct((slots, keys), BF16),
            jax.ShapeDtypeStruct((slots, keys), BF16),
            jax.ShapeDtypeStruct((nbat, half * kloc, 2 * npt), BF16),
            jax.ShapeDtypeStruct((nbat, kloc, npt, LANES), BF16),
            jax.ShapeDtypeStruct((blk_dev, slots), BF16),
            jax.ShapeDtypeStruct((1, 1), jnp.int32),
        ),
        in_specs=[SMEM, VMEM, VMEM, VMEM],
        out_specs=(VMEM,) * 7 + (SMEM,),
    )(task_counts, tasks[0, 0], basis_vals, hot)

    partial = kernel_call(
        density_kernel,
        "density",
        16,
        out_shape=jax.ShapeDtypeStruct((nbat, npt), F32),
        in_specs=[SMEM, VMEM, VMEM, HBM, HBM, HBM],
        out_specs=VMEM,
        scratch_shapes=[
            pltpu.VMEM(counts.shape, BF16),
            pltpu.VMEM(basis_vals.shape, BF16),
            pltpu.VMEM(v2.shape, BF16),
        ]
        + [pltpu.VMEM((nbat * kloc, half * SUB, LANES), BF16)] * 2
        + [pltpu.SemaphoreType.DMA((3,))],
    )(flag, received, counts, in_hbm(counts_hi), in_hbm(basis_vals), in_hbm(v2))
    swap = [(0, 1), (1, 0)]
    other = lax.ppermute(partial, "blk", swap)

    slot_sums, density = kernel_call(
        potential_kernel,
        "potential",
        24,
        out_shape=(wide, jax.ShapeDtypeStruct((nbat, npt), F32)),
        in_specs=[SMEM, VMEM, VMEM, VMEM, HBM, VMEM, VMEM],
        out_specs=(VMEM, VMEM),
        scratch_shapes=[
            pltpu.VMEM((half, keys, LANES), BF16),
            pltpu.VMEM((nbat, 2 * npt), F32),
            pltpu.VMEM(counts_t.shape, BF16),
            pltpu.SemaphoreType.DMA((1,)),
        ],
    )(flag, partial, other, counts_t, in_hbm(counts_t_hi), vt, v2)
    returned = exchange(slot_sums)

    owner_sums = kernel_call(
        owner_kernel,
        "owner",
        8,
        out_shape=jax.ShapeDtypeStruct((blk_dev, bs, bs), F32),
        in_specs=[VMEM, VMEM],
        out_specs=VMEM,
    )(hot_t, returned)
    return (density, owner_sums[None])


def solution(mesh):
    in_specs = (
        P("blk", "slab", None, None),
        P("slab", None, None, None),
        P("blk", "slab", None, None),
        P("blk", "slab", None, None),
        P("blk", "slab"),
    )
    out_specs = (P("slab", None), P("blk", "slab", None, None))
    return jax.shard_map(body, mesh=mesh, in_specs=in_specs, out_specs=out_specs, check_vma=False)
```
